256 devices in a mesh: req: 64 (over y, z, core), rep: 4 (over x).
Axes of the slice: x: 4, y: 4, z: 8, core: 2. Of those that a mesh axis runs over, the one named last changes fastest.
Arguments:
- hidden: bfloat16 [512, 64, 1152], P('rep', 'req'), may hold values from -6 to 6
- norm_gain: float32 [1152], replicated, may hold values from 0.1 to 1.9
- w_qkv: bfloat16 [1152, 1920], replicated, may hold values from -0.1875 to 0.1875
- w_out: bfloat16 [1152, 1152], replicated, may hold values from -0.1875 to 0.1875
- ffn_gain: float32 [1152], replicated, may hold values from 0.1 to 1.9
- w_gate: bfloat16 [1152, 1536], P(None, 'rep'), may hold values from -0.1875 to 0.1875
- w_up: bfloat16 [1152, 1536], P(None, 'rep'), may hold values from -0.1875 to 0.1875
- w_down: bfloat16 [1536, 1152], P('rep'), may hold values from -0.15625 to 0.15625
- cache: bfloat16 [4096, 2, 128, 384], P(('req', 'rep')), may hold values from -363 to 363, as said below
- page_table: int32 [512, 4, 5], P('req', 'rep'), may hold values from 0 to 15, as said below
- cache_len: int32 [512], P('req'), may hold values from 2049 to 2560, as said below
- parents: int32 [512, 64], P('req'), may hold values from 0 to 62, as said below
- accept_leaf: int32 [512], P('req'), may hold values from 0 to 63, as said below
- page_slot: int32 [512], P('req'), may hold values from 0 to 7, as said below
Outputs:
- out: bfloat16 [512, 64, 1152], P('rep', 'req')
- new_pages: bfloat16 [512, 2, 8, 384], P(('req', 'rep'))
The draws below stay inside these ranges and needn't reach their ends.
Inputs may be any that keep to these rules, and one draw needn't show every extreme that they name: `cache`: no structure is promised. page_table[r, j, s] is the index, among the 16 pages of device j of request r's owner, of the request's logical page s * 4 + j; requests of one owner in aligned blocks of 4 share the pages of logical pages below 16; all other pages are distinct. `cache_len`: every owner holds a request of the largest length. parents[r, 0] = 0; node t >= 1 has depth (t * 7 + 62) // 63 and its parent is a node of the depth before. accept_leaf names a node of depth 8 - 1. `page_slot`: the 8 requests of each owner take each slot once.
All inputs are finite; a program needn't handle non-finite values.
Results may differ from the reference program's by a relative error of at most 0.019.
The reference program's roundings to bfloat16 on the way count: a program that leaves them out, or rounds other values in their place, can miss the bound.
Values may be sent and summed in bfloat16 or wider, within the bound.
A program may use at most 128 MiB of HBM per device.

```python
import jax
import jax.numpy as jnp
from jax import lax

D = 1152
QUERY_HEADS = 18
KEY_VALUE_HEADS = 6
HEAD_SIZE = 64
FF = 1536
QUERY_COLUMNS = 1152
KEY_VALUE_WIDTH = 384
DRAFT_TOKENS = 64
ACC = 8
PAGE_ENTRIES = 128
PRE = 16
PRIV = 4
GROUP = 4
REQ_DEV = 8
OWNERS = 64
REPLICA_DEVICES = 4
R = 512
PAGE_SLOTS = 5
PG_DEV = 16
NPG = 4096


def tree_levels():
    node_ids = jnp.arange(DRAFT_TOKENS, dtype=jnp.int32)
    return (node_ids * (ACC - 1) + DRAFT_TOKENS - 2) // (DRAFT_TOKENS - 1)


def draw_cache(key, part):
    entries = jax.random.truncated_normal(key, -4.5, 4.5, (NPG, 2, PAGE_ENTRIES, KEY_VALUE_WIDTH), jnp.float32)
    offsets = jax.random.truncated_normal(jax.random.fold_in(key, 3), -4.5, 4.5, (NPG, 1, 1, KEY_VALUE_WIDTH), jnp.float32) * 2.5
    value_part = (jnp.arange(2) == 1).astype(jnp.float32)[None, :, None, None]
    entries = entries + offsets * value_part
    return entries.astype(jnp.bfloat16)


def draw_page_table(key, part):
    scores = jax.random.randint(key, (OWNERS, REPLICA_DEVICES, PG_DEV), 0, 1 << 20) * PG_DEV + jnp.arange(PG_DEV, dtype=jnp.int32)
    shuffled = jnp.argsort(scores, axis=-1).astype(jnp.int32)
    request_ids = jnp.arange(REQ_DEV, dtype=jnp.int32)[:, None, None]
    rep_ids = jnp.arange(REPLICA_DEVICES, dtype=jnp.int32)[None, :, None]
    slot_ids = jnp.arange(PAGE_SLOTS, dtype=jnp.int32)[None, None, :]
    logical = slot_ids * REPLICA_DEVICES + rep_ids
    shared_slots = PRE // REPLICA_DEVICES
    local_ids = jnp.where(logical < PRE, request_ids // GROUP * shared_slots + slot_ids, REQ_DEV // GROUP * shared_slots + request_ids * (PRIV // REPLICA_DEVICES) + slot_ids - shared_slots)
    local_ids = jnp.broadcast_to(local_ids, (REQ_DEV, REPLICA_DEVICES, PAGE_SLOTS))
    table = jnp.take_along_axis(shuffled[:, None, :, :], local_ids[None, :, :, :], axis=-1)
    return table.reshape(R, REPLICA_DEVICES, PAGE_SLOTS).astype(jnp.int32)


def draw_cache_len(key, part):
    shortest = PRE * PAGE_ENTRIES + 1
    longest_len = (PRE + PRIV) * PAGE_ENTRIES
    lengths = jax.random.randint(key, (OWNERS, REQ_DEV), shortest, longest_len + 1)
    longest = jax.random.randint(jax.random.fold_in(key, 7), (OWNERS, 1), 0, REQ_DEV)
    lengths = jnp.where(jnp.arange(REQ_DEV)[None, :] == longest, longest_len, lengths)
    return lengths.reshape(R).astype(jnp.int32)


def draw_parents(key, part):
    levels = tree_levels()
    lower_bound = jnp.sum(levels[None, :] < levels[:, None] - 1, axis=1)
    upper_bound = jnp.sum(levels[None, :] < levels[:, None], axis=1)
    upper_bound = jnp.maximum(upper_bound, lower_bound + 1)
    chosen = jax.random.randint(key, (R, DRAFT_TOKENS), lower_bound[None, :], upper_bound[None, :])
    return chosen.astype(jnp.int32)


def draw_accept_leaf(key, part):
    levels = tree_levels()
    first_leaf = jnp.sum(levels < ACC - 1)
    return jax.random.randint(key, (R,), first_leaf, DRAFT_TOKENS).astype(jnp.int32)


def draw_page_slot(key, part):
    scores = jax.random.randint(key, (OWNERS, REQ_DEV), 0, 1 << 20) * REQ_DEV + jnp.arange(REQ_DEV, dtype=jnp.int32)
    return jnp.argsort(scores, axis=-1).reshape(R).astype(jnp.int32)


def block_scale(key, extent, cuts, least, high):
    factor_of = 1.0
    for dim, shards_of in cuts:
        steps = jax.random.uniform(jax.random.fold_in(jax.random.fold_in(key, 6), dim), (shards_of,), jnp.float32, least / len(cuts), high / len(cuts))
        factor_of = factor_of * jnp.repeat(jnp.exp(steps), extent[dim] // shards_of).reshape((-1,) + (1,) * (len(extent) - 1 - dim))
    return factor_of


def gaussian(rng, dims, spread, reach, cuts=(), held_as=jnp.bfloat16):
    values = spread * jax.random.normal(rng, dims, jnp.float32)
    if cuts:
        values = values * block_scale(rng, dims, cuts, -0.22, 0.18)
    return jnp.clip(values, -reach, reach).astype(held_as)


def setup_inputs(seed: int = 0) -> dict:
    seeds = jax.random.split(jax.random.key(seed), 15)
    return {
        "hidden": gaussian(seeds[0], (R, DRAFT_TOKENS, D), 1.0, 6.0, ((0, 4), (1, 64))),
        "norm_gain": jnp.clip(1.0 + 0.18 * jax.random.normal(seeds[1], (D,), jnp.float32), 0.1, 1.9),
        "w_qkv": gaussian(seeds[2], (D, QUERY_COLUMNS + 2 * KEY_VALUE_WIDTH), D ** -0.5, 0.1875),
        "w_out": gaussian(seeds[3], (QUERY_COLUMNS, D), QUERY_COLUMNS ** -0.5, 0.1875),
        "ffn_gain": jnp.clip(1.0 + 0.18 * jax.random.normal(seeds[4], (D,), jnp.float32), 0.1, 1.9),
        "w_gate": gaussian(seeds[5], (D, FF), D ** -0.5, 0.1875, ((1, 4),)),
        "w_up": gaussian(seeds[6], (D, FF), D ** -0.5, 0.1875, ((1, 4),)),
        "w_down": gaussian(seeds[7], (FF, D), FF ** -0.5, 0.15625, ((0, 4),)),
        "cache": draw_cache(jax.random.fold_in(seeds[14], 71), 0),
        "page_table": draw_page_table(jax.random.fold_in(seeds[14], 71), 0),
        "cache_len": draw_cache_len(jax.random.fold_in(seeds[14], 71), 0),
        "parents": draw_parents(jax.random.fold_in(seeds[14], 71), 0),
        "accept_leaf": draw_accept_leaf(jax.random.fold_in(seeds[14], 71), 0),
        "page_slot": draw_page_slot(jax.random.fold_in(seeds[14], 71), 0),
    }


SCALE = 0.125
EPSILON = 1e-05
THETA = 10000.0

def apply_rotation(values, token_positions, head_count):
    head_columns = values.shape[-1] // head_count
    half_width = head_columns // 2
    shaped = values.reshape(values.shape[:-1] + (head_count, head_columns))
    frequency = THETA ** (-jnp.arange(half_width, dtype=jnp.float32) / half_width)
    angles = token_positions.astype(jnp.float32)[..., None] * frequency
    cosine = jnp.cos(angles)[..., None, :]
    sines = jnp.sin(angles)[..., None, :]
    front_half = shaped[..., :half_width]
    back_half = shaped[..., half_width:]
    turned = jnp.concatenate([front_half * cosine - back_half * sines, back_half * cosine + front_half * sines], axis=-1)
    return turned.reshape(values.shape)

def ancestors(parents):
    tree_length = parents.shape[-1]
    identity = jnp.eye(tree_length, dtype=jnp.float32)
    linked = jax.nn.one_hot(parents, tree_length, dtype=jnp.float32)
    reached = jnp.minimum(identity + linked, 1.0)
    for doubling in range(tree_length.bit_length()):
        reached = jnp.minimum(jnp.einsum('rts,rsu->rtu', reached, reached, precision=lax.Precision.HIGHEST), 1.0)
    return reached

def reference(hidden, norm_gain, w_qkv, w_out, ffn_gain, w_gate, w_up, w_down, cache, page_table, cache_len, parents, accept_leaf, page_slot):
    values_in = hidden.astype(jnp.float32)
    scaling = lax.rsqrt(lax.optimization_barrier(jnp.mean(values_in * values_in, axis=-1, keepdims=True)) + EPSILON)
    normed = (values_in * scaling * norm_gain).astype(jnp.bfloat16)
    projected_rows = jnp.dot(normed.reshape(R * DRAFT_TOKENS, D), w_qkv, preferred_element_type=jnp.float32).astype(jnp.bfloat16)
    projected_rows = projected_rows.reshape(REQ_DEV, OWNERS, DRAFT_TOKENS, QUERY_COLUMNS + 2 * KEY_VALUE_WIDTH).transpose(1, 0, 2, 3).reshape(R, DRAFT_TOKENS, QUERY_COLUMNS + 2 * KEY_VALUE_WIDTH)
    reached = ancestors(parents)
    depths = lax.optimization_barrier(jnp.sum(reached, axis=-1)).astype(jnp.int32) - 1
    token_positions = cache_len[:, None] + depths
    queries = apply_rotation(projected_rows[..., :QUERY_COLUMNS].astype(jnp.float32), token_positions, QUERY_HEADS).astype(jnp.bfloat16)
    key_matrix = apply_rotation(projected_rows[..., QUERY_COLUMNS:QUERY_COLUMNS + KEY_VALUE_WIDTH].astype(jnp.float32), token_positions, KEY_VALUE_HEADS).astype(jnp.bfloat16)
    value_matrix = projected_rows[..., QUERY_COLUMNS + KEY_VALUE_WIDTH:]
    owner_ids = jnp.arange(R, dtype=jnp.int32) // REQ_DEV
    logical = ((jnp.arange(PAGE_SLOTS, dtype=jnp.int32)[None, :] * REPLICA_DEVICES + jnp.arange(REPLICA_DEVICES, dtype=jnp.int32)[:, None]) * PAGE_ENTRIES)[:, :, None] + jnp.arange(PAGE_ENTRIES, dtype=jnp.int32)[None, None, :]
    logical = logical.reshape(REPLICA_DEVICES * PAGE_SLOTS * PAGE_ENTRIES)
    heads_per_group = QUERY_HEADS // KEY_VALUE_HEADS

    def per_request(request_item):
        query_matrix, tree_keys, tree_values, reach_rows, page_list, cache_end, owner_id = request_item
        global_ids = (owner_id * REPLICA_DEVICES + jnp.arange(REPLICA_DEVICES, dtype=jnp.int32)[:, None]) * PG_DEV + page_list
        collected_pages = cache[global_ids]
        stored_keys = collected_pages[:, :, 0].reshape(REPLICA_DEVICES * PAGE_SLOTS * PAGE_ENTRIES, KEY_VALUE_HEADS, HEAD_SIZE)
        stored_values = collected_pages[:, :, 1].reshape(REPLICA_DEVICES * PAGE_SLOTS * PAGE_ENTRIES, KEY_VALUE_HEADS, HEAD_SIZE)
        merged_keys = jnp.concatenate([stored_keys, tree_keys.reshape(DRAFT_TOKENS, KEY_VALUE_HEADS, HEAD_SIZE)], axis=0).astype(jnp.float32)
        merged_values = jnp.concatenate([stored_values, tree_values.reshape(DRAFT_TOKENS, KEY_VALUE_HEADS, HEAD_SIZE)], axis=0).astype(jnp.float32)
        visible = jnp.broadcast_to((logical < cache_end)[None, :], (DRAFT_TOKENS, REPLICA_DEVICES * PAGE_SLOTS * PAGE_ENTRIES))
        allowed = jnp.concatenate([visible, reach_rows > 0.5], axis=1)
        grouped_queries = query_matrix.astype(jnp.float32).reshape(DRAFT_TOKENS, KEY_VALUE_HEADS, heads_per_group, HEAD_SIZE)
        scores = jnp.einsum('tgrd,sgd->gtrs', grouped_queries, merged_keys) * SCALE
        scores = jnp.where(allowed[None, :, None, :], scores, -jnp.inf)
        peaks = lax.optimization_barrier(jnp.max(scores, axis=-1))
        weights = jnp.exp(scores - peaks[..., None])
        totals = lax.optimization_barrier(jnp.sum(weights, axis=-1))
        rounded = lax.optimization_barrier(weights.astype(jnp.bfloat16)).astype(jnp.float32)
        summed = jnp.einsum('gtrs,sgd->tgrd', rounded, merged_values)
        result = summed / jnp.transpose(totals, (1, 0, 2))[..., None]
        return result.reshape(DRAFT_TOKENS, QUERY_COLUMNS).astype(jnp.bfloat16)
    attended = lax.map(per_request, (queries, key_matrix, value_matrix, reached, page_table, cache_len, owner_ids))
    attended = attended.reshape(OWNERS, REQ_DEV, DRAFT_TOKENS, QUERY_COLUMNS).transpose(1, 0, 2, 3).reshape(R * DRAFT_TOKENS, QUERY_COLUMNS)
    residual = (jnp.dot(attended, w_out, preferred_element_type=jnp.float32) + values_in.reshape(R * DRAFT_TOKENS, D)).astype(jnp.bfloat16)
    residual_wide = residual.astype(jnp.float32)
    ffn_scaling = lax.rsqrt(lax.optimization_barrier(jnp.mean(residual_wide * residual_wide, axis=-1, keepdims=True)) + EPSILON)
    ffn_in = (residual_wide * ffn_scaling * ffn_gain).astype(jnp.bfloat16)
    gate = jnp.dot(ffn_in, w_gate, preferred_element_type=jnp.float32)
    up = jnp.dot(ffn_in, w_up, preferred_element_type=jnp.float32)
    activated = (jax.nn.silu(gate) * up).astype(jnp.bfloat16)
    out = (jnp.dot(activated, w_down, preferred_element_type=jnp.float32) + residual_wide).reshape(R, DRAFT_TOKENS, D).astype(jnp.bfloat16)
    leaf_hot = jax.nn.one_hot(accept_leaf, DRAFT_TOKENS, dtype=jnp.float32)
    on_path = jnp.einsum('rt,rts->rs', leaf_hot, reached, precision=lax.Precision.HIGHEST)
    level_hot = (depths[:, None, :] == jnp.arange(ACC, dtype=jnp.int32)[None, :, None]).astype(jnp.float32)
    selector = on_path[:, None, :] * level_hot
    stacked = jnp.stack([key_matrix, value_matrix], axis=1).astype(jnp.float32)
    rows = jnp.einsum('ras,rbsc->rbac', selector, stacked, precision=lax.Precision.HIGHEST).astype(jnp.bfloat16)
    destination = owner_ids * REQ_DEV + page_slot
    new_pages = jnp.zeros((R, 2, ACC, KEY_VALUE_WIDTH), jnp.bfloat16).at[destination].set(rows)
    return (out, new_pages)
```

```python
import functools

import jax
import jax.numpy as jnp
from jax import lax
from jax.experimental import pallas as pl
from jax.experimental.pallas import tpu as pltpu
from jax.sharding import PartitionSpec as P

QUERY_HEADS = 18
KEY_VALUE_HEADS = 6
ACC = 8


SCALE = 0.125
EPSILON = 1e-05
THETA = 10000.0


def apply_rotation(values, token_positions, head_count):
    head_columns = values.shape[-1] // head_count
    half_width = head_columns // 2
    shaped = values.reshape(values.shape[:-1] + (head_count, head_columns))
    frequency = THETA ** (-jnp.arange(half_width, dtype=jnp.float32) / half_width)
    angles = token_positions.astype(jnp.float32)[..., None] * frequency
    cosine = jnp.cos(angles)[..., None, :]
    sines = jnp.sin(angles)[..., None, :]
    front_half = shaped[..., :half_width]
    back_half = shaped[..., half_width:]
    turned = jnp.concatenate(
        [front_half * cosine - back_half * sines, back_half * cosine + front_half * sines], axis=-1
    )
    return turned.reshape(values.shape)


def ancestors(parents):
    tree_length = parents.shape[-1]
    identity = jnp.eye(tree_length, dtype=jnp.float32)
    linked = jax.nn.one_hot(parents, tree_length, dtype=jnp.float32)
    reached = jnp.minimum(identity + linked, 1.0)
    for doubling in range(tree_length.bit_length()):
        reached = jnp.minimum(
            jnp.einsum("rts,rsu->rtu", reached, reached, precision=lax.Precision.HIGHEST), 1.0
        )
    return reached


def rms_scaled(values_in, gain):
    scaling = lax.rsqrt(jnp.mean(values_in * values_in, axis=-1, keepdims=True) + EPSILON)
    return (values_in * scaling * gain).astype(jnp.bfloat16)


def path_rows(key_matrix, value_matrix, reached, depths, leaf_ids):
    tree_length = reached.shape[-1]
    leaf_hot = jax.nn.one_hot(leaf_ids, tree_length, dtype=jnp.float32)
    on_path = jnp.einsum("rt,rts->rs", leaf_hot, reached, precision=lax.Precision.HIGHEST)
    level_hot = (depths[:, None, :] == jnp.arange(ACC, dtype=jnp.int32)[None, :, None]).astype(
        jnp.float32
    )
    selector = (on_path[:, None, :] * level_hot).astype(jnp.bfloat16)
    stacked = jnp.stack([key_matrix, value_matrix], axis=1)
    return jnp.einsum(
        "ras,rbsc->rbac", selector, stacked, preferred_element_type=jnp.float32
    ).astype(jnp.bfloat16)


def place_rows(rows, page_slot, own_start, owner_page_count):
    slot_ids = own_start + jnp.arange(owner_page_count, dtype=jnp.int32)
    chooser = (page_slot[None, :] == slot_ids[:, None]).astype(jnp.bfloat16)
    return jnp.einsum("pr,rbac->pbac", chooser, rows, preferred_element_type=jnp.float32).astype(
        jnp.bfloat16
    )


def paged_kernel(slots, chunks, page_ref, limit_ref, *refs):
    q_ref = refs[0]
    page_refs = refs[1 : 1 + slots]
    dk_ref, dv_ref, dmask_ref = refs[1 + slots : 4 + slots]
    m_ref, l_ref, acc_ref = refs[4 + slots :]
    request = pl.program_id(0)
    rows = q_ref.shape[2]
    page_length = page_refs[0].shape[2]
    lane_ids = lax.broadcasted_iota(jnp.int32, (rows, page_length), 1)
    draft_open = dmask_ref[0] > 0.5
    nt = (((1,), (1,)), ((), ()))
    for c in range(chunks):
        lanes = pl.ds(c * 128, 128)
        qc = q_ref[0, c]
        parts = []
        for s in range(slots):
            kc = page_refs[s][0, 0, :, lanes]
            sc = lax.dot_general(qc, kc, nt, preferred_element_type=jnp.float32) * SCALE
            sc = jnp.where(lane_ids < limit_ref[request, s], sc, -jnp.inf)
            parts.append(sc)
        kd = dk_ref[0, :, lanes]
        sd = lax.dot_general(qc, kd, nt, preferred_element_type=jnp.float32) * SCALE
        sd = jnp.where(draft_open, sd, -jnp.inf)
        peak = jnp.max(sd, axis=-1, keepdims=True)
        for sc in parts:
            peak = jnp.maximum(peak, jnp.max(sc, axis=-1, keepdims=True))
        wd = jnp.exp(sd - peak)
        total = jnp.sum(wd, axis=-1, keepdims=True)
        acc = jnp.dot(
            wd.astype(jnp.bfloat16), dv_ref[0, :, lanes], preferred_element_type=jnp.float32
        )
        for s in range(slots):
            ws = jnp.exp(parts[s] - peak)
            total = total + jnp.sum(ws, axis=-1, keepdims=True)
            acc = acc + jnp.dot(
                ws.astype(jnp.bfloat16),
                page_refs[s][0, 1, :, lanes],
                preferred_element_type=jnp.float32,
            )
        m_ref[0, c] = peak
        l_ref[0, c] = total
        acc_ref[0, c] = acc


def paged_partials(q2, cache, page_list, limits, draft_keys, draft_values, draft_mask):
    requests, chunks, rows, lanes = q2.shape
    slots = page_list.shape[1]
    page_length = cache.shape[2]
    width = cache.shape[3]
    tree_length = draft_keys.shape[1]

    def page_map(s):
        return lambda k, pages, limit: (pages[k, s], 0, 0, 0)

    in_specs = [pl.BlockSpec((1, chunks, rows, lanes), lambda k, pages, limit: (k, 0, 0, 0))]
    in_specs += [pl.BlockSpec((1, 2, page_length, width), page_map(s)) for s in range(slots)]
    in_specs += [
        pl.BlockSpec((1, tree_length, width), lambda k, pages, limit: (k, 0, 0)),
        pl.BlockSpec((1, tree_length, width), lambda k, pages, limit: (k, 0, 0)),
        pl.BlockSpec((1, rows, tree_length), lambda k, pages, limit: (k, 0, 0)),
    ]
    out_specs = [
        pl.BlockSpec((1, chunks, rows, 1), lambda k, pages, limit: (k, 0, 0, 0)),
        pl.BlockSpec((1, chunks, rows, 1), lambda k, pages, limit: (k, 0, 0, 0)),
        pl.BlockSpec((1, chunks, rows, lanes), lambda k, pages, limit: (k, 0, 0, 0)),
    ]
    out_shape = [
        jax.ShapeDtypeStruct((requests, chunks, rows, 1), jnp.float32),
        jax.ShapeDtypeStruct((requests, chunks, rows, 1), jnp.float32),
        jax.ShapeDtypeStruct((requests, chunks, rows, lanes), jnp.float32),
    ]
    keys_seen = slots * page_length + tree_length
    cost = pl.CostEstimate(
        flops=requests * chunks * rows * lanes * keys_seen * 4,
        bytes_accessed=requests * (slots * 2 * page_length * width * 2 + chunks * rows * lanes * 6),
        transcendentals=requests * chunks * rows * keys_seen,
    )
    grid_spec = pltpu.PrefetchScalarGridSpec(
        num_scalar_prefetch=2,
        grid=(requests,),
        in_specs=in_specs,
        out_specs=out_specs,
    )
    return pl.pallas_call(
        functools.partial(paged_kernel, slots, chunks),
        grid_spec=grid_spec,
        out_shape=out_shape,
        cost_estimate=cost,
        compiler_params=pltpu.CompilerParams(dimension_semantics=("arbitrary",)),
        name="paged_partials",
    )(page_list, limits, q2, *([cache] * slots), draft_keys, draft_values, draft_mask)


def pair_queries(queries, requests, tree_length):
    head_columns = queries.shape[-1] // QUERY_HEADS
    group = QUERY_HEADS // KEY_VALUE_HEADS
    chunks = KEY_VALUE_HEADS // 2
    shaped = queries.reshape(requests, tree_length, chunks, 2, group, head_columns)
    shaped = shaped.transpose(0, 2, 3, 1, 4, 5).reshape(
        requests, chunks, 2, tree_length * group, head_columns
    )
    zeros = jnp.zeros_like(shaped[:, :, 0])
    top = jnp.concatenate([shaped[:, :, 0], zeros], axis=-1)
    bottom = jnp.concatenate([zeros, shaped[:, :, 1]], axis=-1)
    return jnp.concatenate([top, bottom], axis=2)


def unpair_rows(values, requests, tree_length):
    group = QUERY_HEADS // KEY_VALUE_HEADS
    chunks = KEY_VALUE_HEADS // 2
    shaped = values.reshape(requests, chunks, 2, tree_length, group)
    return shaped.transpose(0, 3, 1, 2, 4).reshape(requests, tree_length, QUERY_HEADS)


def unpair_sums(acc, requests, tree_length):
    group = QUERY_HEADS // KEY_VALUE_HEADS
    chunks = KEY_VALUE_HEADS // 2
    head_columns = acc.shape[-1] // 2
    shaped = acc.reshape(requests, chunks, 2, tree_length, group, 2, head_columns)
    diagonal = jnp.stack([shaped[:, :, 0, :, :, 0], shaped[:, :, 1, :, :, 1]], axis=2)
    return diagonal.transpose(0, 3, 1, 2, 4, 5).reshape(
        requests, tree_length, QUERY_HEADS * head_columns
    )


def body(
    hidden,
    norm_gain,
    w_qkv,
    w_out,
    ffn_gain,
    w_gate,
    w_up,
    w_down,
    cache,
    page_table,
    cache_len,
    parents,
    accept_leaf,
    page_slot,
):
    block_rows, draft_part, model_width = hidden.shape
    channels = w_qkv.shape[1]
    query_columns = w_out.shape[0]
    key_value_columns = (channels - query_columns) // 2
    req_count = lax.axis_size("req")
    rep_count = lax.axis_size("rep")
    rep_index = lax.axis_index("rep")
    requests = cache_len.shape[0]
    owner_page_count = requests // rep_count
    tree_length = parents.shape[1]
    own_start = rep_index * owner_page_count
    page_length = cache.shape[2]
    slots_count = page_table.shape[2]

    local_rows = hidden.reshape(owner_page_count, req_count, model_width)
    own_hidden = lax.all_to_all(local_rows, "req", split_axis=1, concat_axis=1, tiled=True)
    all_hidden = lax.all_gather(own_hidden, "rep", axis=0, tiled=True)

    normed = rms_scaled(all_hidden.astype(jnp.float32), norm_gain)
    projected = jnp.dot(
        normed.reshape(-1, model_width), w_qkv, preferred_element_type=jnp.float32
    ).astype(jnp.bfloat16).reshape(requests, tree_length, channels)

    reached = ancestors(parents)
    depths = jnp.sum(reached, axis=-1).astype(jnp.int32) - 1
    token_positions = cache_len[:, None] + depths
    queries = apply_rotation(
        projected[..., :query_columns].astype(jnp.float32), token_positions, QUERY_HEADS
    ).astype(jnp.bfloat16)
    keys_all = apply_rotation(
        projected[..., query_columns : query_columns + key_value_columns].astype(jnp.float32),
        token_positions,
        KEY_VALUE_HEADS,
    ).astype(jnp.bfloat16)
    values_all = projected[..., query_columns + key_value_columns :]

    group = QUERY_HEADS // KEY_VALUE_HEADS
    q2 = pair_queries(queries, requests, tree_length)
    page_list = page_table[:, 0, :]
    starts = (
        jnp.arange(slots_count, dtype=jnp.int32)[None, :] * rep_count + rep_index
    ) * page_length
    limits = cache_len[:, None] - starts
    mine = (jnp.arange(requests, dtype=jnp.int32) // owner_page_count) == rep_index
    open_rows = jnp.where(mine[:, None, None], reached, 0.0)
    open_rows = jnp.repeat(open_rows, group, axis=1)
    draft_mask = jnp.concatenate([open_rows, open_rows], axis=1)
    peaks, totals, sums = paged_partials(
        q2, cache, page_list, limits, keys_all, values_all, draft_mask
    )
    peaks = unpair_rows(peaks, requests, tree_length)
    totals = unpair_rows(totals, requests, tree_length)
    sums = unpair_sums(sums, requests, tree_length)

    peak_all = lax.pmax(peaks, "rep")
    factors = jnp.exp(peaks - peak_all)
    scaled = (sums.reshape(requests, tree_length, QUERY_HEADS, -1) * factors[..., None]).reshape(
        requests, tree_length, query_columns
    )
    joined = jnp.concatenate([scaled, totals * factors], axis=-1)
    shared = lax.psum_scatter(joined, "rep", scatter_dimension=0, tiled=True)
    attended = (
        (
            shared[..., :query_columns].reshape(owner_page_count, tree_length, QUERY_HEADS, -1)
            / shared[..., query_columns:][..., None]
        )
        .reshape(-1, query_columns)
        .astype(jnp.bfloat16)
    )

    mixed = jnp.dot(attended, w_out, preferred_element_type=jnp.float32)
    residual = (mixed + own_hidden.reshape(-1, model_width).astype(jnp.float32)).astype(
        jnp.bfloat16
    )
    residual_wide = residual.astype(jnp.float32)
    ffn_in = rms_scaled(residual_wide, ffn_gain).reshape(owner_page_count, tree_length, model_width)
    rows_in = lax.all_gather(ffn_in, "rep", axis=0, tiled=True).reshape(-1, model_width)
    gate = jnp.dot(rows_in, w_gate, preferred_element_type=jnp.float32)
    up = jnp.dot(rows_in, w_up, preferred_element_type=jnp.float32)
    activated = (jax.nn.silu(gate) * up).astype(jnp.bfloat16)
    ffn_sum = lax.psum_scatter(
        jnp.dot(activated, w_down, preferred_element_type=jnp.float32).reshape(
            requests, tree_length, model_width
        ),
        "rep",
        scatter_dimension=0,
        tiled=True,
    )
    out_own = (ffn_sum + residual_wide.reshape(owner_page_count, tree_length, model_width)).astype(
        jnp.bfloat16
    )
    out = lax.all_to_all(out_own, "req", split_axis=1, concat_axis=1, tiled=True)
    out = out.reshape(block_rows, draft_part, model_width)

    all_rows = path_rows(keys_all, values_all, reached, depths, accept_leaf)
    new_pages = place_rows(all_rows, page_slot, own_start, owner_page_count)
    return (out, new_pages)


def solution(mesh):
    placed = (
        P("rep", "req", None),
        P(),
        P(),
        P(),
        P(),
        P(None, "rep"),
        P(None, "rep"),
        P("rep", None),
        P(("req", "rep"), None, None, None),
        P("req", "rep", None),
        P("req"),
        P("req", None),
        P("req"),
        P("req"),
    )
    return jax.shard_map(
        body,
        mesh=mesh,
        in_specs=placed,
        out_specs=(P("rep", "req", None), P(("req", "rep"), None, None, None)),
        check_vma=False,
    )
```

```python
import functools

import jax
import jax.numpy as jnp
from jax import lax
from jax.experimental import pallas as pl
from jax.experimental.pallas import tpu as pltpu
from jax.sharding import PartitionSpec as P

QUERY_HEADS = 18
KEY_VALUE_HEADS = 6
ACC = 8


SCALE = 0.125
EPSILON = 1e-05
THETA = 10000.0


def apply_rotation(values, token_positions, head_count):
    head_columns = values.shape[-1] // head_count
    half_width = head_columns // 2
    shaped = values.reshape(values.shape[:-1] + (head_count, head_columns))
    frequency = THETA ** (-jnp.arange(half_width, dtype=jnp.float32) / half_width)
    angles = token_positions.astype(jnp.float32)[..., None] * frequency
    cosine = jnp.cos(angles)[..., None, :]
    sines = jnp.sin(angles)[..., None, :]
    front_half = shaped[..., :half_width]
    back_half = shaped[..., half_width:]
    turned = jnp.concatenate(
        [front_half * cosine - back_half * sines, back_half * cosine + front_half * sines], axis=-1
    )
    return turned.reshape(values.shape)


def ancestors(parents):
    tree_length = parents.shape[-1]
    identity = jnp.eye(tree_length, dtype=jnp.float32)
    linked = jax.nn.one_hot(parents, tree_length, dtype=jnp.float32)
    reached = jnp.minimum(identity + linked, 1.0)
    for doubling in range(tree_length.bit_length()):
        reached = jnp.minimum(
            jnp.einsum("rts,rsu->rtu", reached, reached, precision=lax.Precision.HIGHEST), 1.0
        )
    return reached


def rms_scaled(values_in, gain):
    scaling = lax.rsqrt(jnp.mean(values_in * values_in, axis=-1, keepdims=True) + EPSILON)
    return (values_in * scaling * gain).astype(jnp.bfloat16)


def path_rows(key_matrix, value_matrix, reached, depths, leaf_ids):
    tree_length = reached.shape[-1]
    leaf_hot = jax.nn.one_hot(leaf_ids, tree_length, dtype=jnp.float32)
    on_path = jnp.einsum("rt,rts->rs", leaf_hot, reached, precision=lax.Precision.HIGHEST)
    level_hot = (depths[:, None, :] == jnp.arange(ACC, dtype=jnp.int32)[None, :, None]).astype(
        jnp.float32
    )
    selector = (on_path[:, None, :] * level_hot).astype(jnp.bfloat16)
    stacked = jnp.stack([key_matrix, value_matrix], axis=1)
    return jnp.einsum(
        "ras,rbsc->rbac", selector, stacked, preferred_element_type=jnp.float32
    ).astype(jnp.bfloat16)


def place_rows(rows, page_slot, own_start, owner_page_count):
    slot_ids = own_start + jnp.arange(owner_page_count, dtype=jnp.int32)
    chooser = (page_slot[None, :] == slot_ids[:, None]).astype(jnp.bfloat16)
    return jnp.einsum("pr,rbac->pbac", chooser, rows, preferred_element_type=jnp.float32).astype(
        jnp.bfloat16
    )


def paged_kernel(slots, chunks, page_ref, limit_ref, *refs):
    q_ref = refs[0]
    page_refs = refs[1 : 1 + slots]
    dk_ref, dv_ref, dmask_ref = refs[1 + slots : 4 + slots]
    acc_ref, stat_ref = refs[4 + slots :]
    request = pl.program_id(0)
    tree_length = q_ref.shape[1]
    page_length = page_refs[0].shape[2]
    rows = 6 * tree_length
    half = rows // 2
    low_t = lax.broadcasted_iota(jnp.int32, (tree_length, 128), 1) < 64
    low_h = lax.broadcasted_iota(jnp.int32, (half, 128), 1) < 64
    key_lanes = lax.broadcasted_iota(jnp.int32, (rows, page_length), 1)
    stat_lanes = lax.broadcasted_iota(jnp.int32, (rows, 128), 1)
    draft_open = jnp.concatenate([dmask_ref[0]] * 6, axis=0) > 0.5
    nt = (((1,), (1,)), ((), ()))
    for c in range(chunks):
        lanes = pl.ds(c * 128, 128)
        tiles = [q_ref[0, :, pl.ds(c * 384 + 128 * j, 128)].astype(jnp.float32) for j in range(3)]
        turned0 = pltpu.roll(tiles[0], 64, 1)
        turned2 = pltpu.roll(tiles[2], 64, 1)
        blocks = [
            jnp.where(low_t, tiles[0], 0.0),
            jnp.where(low_t, turned0, 0.0),
            jnp.where(low_t, tiles[1], 0.0),
            jnp.where(low_t, 0.0, tiles[1]),
            jnp.where(low_t, 0.0, turned2),
            jnp.where(low_t, 0.0, tiles[2]),
        ]
        qc = jnp.concatenate(blocks, axis=0).astype(jnp.bfloat16)
        parts = []
        for s in range(slots):
            kc = page_refs[s][0, 0, :, lanes]
            sc = lax.dot_general(qc, kc, nt, preferred_element_type=jnp.float32) * SCALE
            sc = jnp.where(key_lanes < limit_ref[request, s], sc, -jnp.inf)
            parts.append(sc)
        kd = dk_ref[0, :, lanes]
        sd = lax.dot_general(qc, kd, nt, preferred_element_type=jnp.float32) * SCALE
        sd = jnp.where(draft_open, sd, -jnp.inf)
        peak = jnp.max(sd, axis=-1, keepdims=True)
        for sc in parts:
            peak = jnp.maximum(peak, jnp.max(sc, axis=-1, keepdims=True))
        wd = jnp.exp(sd - peak)
        total = jnp.sum(wd, axis=-1, keepdims=True)
        acc = jnp.dot(
            wd.astype(jnp.bfloat16), dv_ref[0, :, lanes], preferred_element_type=jnp.float32
        )
        for s in range(slots):
            ws = jnp.exp(parts[s] - peak)
            total = total + jnp.sum(ws, axis=-1, keepdims=True)
            acc = acc + jnp.dot(
                ws.astype(jnp.bfloat16),
                page_refs[s][0, 1, :, lanes],
                preferred_element_type=jnp.float32,
            )
        acc_ref[0, c] = jnp.where(low_h, acc[:half], acc[half:])
        stats = jnp.where(stat_lanes == 0, peak, jnp.where(stat_lanes == 1, total, 0.0))
        stat_ref[0, c] = jnp.transpose(stats)[0:8, :]


def paged_partials(queries, cache, page_list, limits, draft_keys, draft_values, draft_mask):
    requests, tree_length, query_columns = queries.shape
    chunks = KEY_VALUE_HEADS // 2
    rows = 6 * tree_length
    slots = page_list.shape[1]
    page_length = cache.shape[2]
    width = cache.shape[3]

    def page_map(s):
        return lambda k, pages, limit: (pages[k, s], 0, 0, 0)

    in_specs = [pl.BlockSpec((1, tree_length, query_columns), lambda k, pages, limit: (k, 0, 0))]
    in_specs += [pl.BlockSpec((1, 2, page_length, width), page_map(s)) for s in range(slots)]
    in_specs += [
        pl.BlockSpec((1, tree_length, width), lambda k, pages, limit: (k, 0, 0)),
        pl.BlockSpec((1, tree_length, width), lambda k, pages, limit: (k, 0, 0)),
        pl.BlockSpec((1, tree_length, tree_length), lambda k, pages, limit: (k, 0, 0)),
    ]
    out_specs = [
        pl.BlockSpec((1, chunks, rows // 2, 128), lambda k, pages, limit: (k, 0, 0, 0)),
        pl.BlockSpec((1, chunks, 8, rows), lambda k, pages, limit: (k, 0, 0, 0)),
    ]
    out_shape = [
        jax.ShapeDtypeStruct((requests, chunks, rows // 2, 128), jnp.float32),
        jax.ShapeDtypeStruct((requests, chunks, 8, rows), jnp.float32),
    ]
    keys_seen = slots * page_length + tree_length
    cost = pl.CostEstimate(
        flops=requests * chunks * rows * 128 * keys_seen * 4,
        bytes_accessed=requests * (slots * 2 * page_length * width * 2 + chunks * rows * 128 * 3),
        transcendentals=requests * chunks * rows * keys_seen,
    )
    grid_spec = pltpu.PrefetchScalarGridSpec(
        num_scalar_prefetch=2,
        grid=(requests,),
        in_specs=in_specs,
        out_specs=out_specs,
    )
    return pl.pallas_call(
        functools.partial(paged_kernel, slots, chunks),
        grid_spec=grid_spec,
        out_shape=out_shape,
        cost_estimate=cost,
        compiler_params=pltpu.CompilerParams(dimension_semantics=("arbitrary",)),
        name="paged_partials",
    )(page_list, limits, queries, *([cache] * slots), draft_keys, draft_values, draft_mask)


def rescale_kernel(acc_ref, stat_ref, peak_ref, out_ref):
    chunks, half = acc_ref.shape[1], acc_ref.shape[2]
    rows = 2 * half
    low_h = lax.broadcasted_iota(jnp.int32, (half, 128), 1) < 64
    for c in range(chunks):
        local_peak = stat_ref[0, c, 0:1, :]
        factor = jnp.exp(local_peak - peak_ref[0, c : c + 1, :])
        scaled_total = stat_ref[0, c, 1:2, :] * factor
        column = jnp.transpose(jnp.broadcast_to(factor, (128, rows)))
        out_ref[0, c, 0:half, :] = acc_ref[0, c] * jnp.where(low_h, column[:half], column[half:])
        pieces = [scaled_total[:, 128 * j : 128 * (j + 1)] for j in range(rows // 128)]
        pieces.append(jnp.zeros((8 - rows // 128, 128), jnp.float32))
        out_ref[0, c, half : half + 8, :] = jnp.concatenate(pieces, axis=0)


def rescale(acc, stats, peak_all):
    requests, chunks, half, lanes = acc.shape
    rows = 2 * half
    return pl.pallas_call(
        rescale_kernel,
        grid=(requests,),
        in_specs=[
            pl.BlockSpec((1, chunks, half, lanes), lambda k: (k, 0, 0, 0)),
            pl.BlockSpec((1, chunks, 8, rows), lambda k: (k, 0, 0, 0)),
            pl.BlockSpec((1, chunks, rows), lambda k: (k, 0, 0)),
        ],
        out_specs=pl.BlockSpec((1, chunks, half + 8, lanes), lambda k: (k, 0, 0, 0)),
        out_shape=jax.ShapeDtypeStruct((requests, chunks, half + 8, lanes), jnp.float32),
        compiler_params=pltpu.CompilerParams(dimension_semantics=("arbitrary",)),
        name="rescale_partials",
    )(acc, stats, peak_all)


def finish_attention(shared, requests, tree_length):
    group = QUERY_HEADS // KEY_VALUE_HEADS
    chunks = shared.shape[1]
    half = group * tree_length
    sums = shared[:, :, :half, :].reshape(requests, chunks, group, tree_length, 2, 64)
    totals = shared[:, :, half : half + 2 * group * tree_length // 128, :].reshape(
        requests, chunks, 2, group, tree_length
    )
    totals = totals.transpose(0, 1, 3, 4, 2)[..., None]
    result = (sums / totals).transpose(0, 3, 1, 4, 2, 5)
    return result.reshape(requests * tree_length, chunks * 2 * group * 64).astype(jnp.bfloat16)


def rotate_flat(values, token_positions, head_columns):
    half_width = head_columns // 2
    frequency = THETA ** (-jnp.arange(half_width, dtype=jnp.float32) / half_width)
    angles = token_positions.astype(jnp.float32)[:, None] * frequency
    cosine = jnp.cos(angles)
    sines = jnp.sin(angles)
    repeats = values.shape[-1] // head_columns
    cosine = jnp.tile(jnp.concatenate([cosine, cosine], axis=-1), (1, repeats))
    sines = jnp.tile(jnp.concatenate([-sines, sines], axis=-1), (1, repeats))
    columns = jnp.arange(values.shape[-1], dtype=jnp.int32)
    front = (columns % head_columns) < half_width
    partner = jnp.where(
        front[None, :], jnp.roll(values, -half_width, axis=-1), jnp.roll(values, half_width, axis=-1)
    )
    return values * cosine + partner * sines


def body(
    hidden,
    norm_gain,
    w_qkv,
    w_out,
    ffn_gain,
    w_gate,
    w_up,
    w_down,
    cache,
    page_table,
    cache_len,
    parents,
    accept_leaf,
    page_slot,
):
    block_rows, draft_part, model_width = hidden.shape
    channels = w_qkv.shape[1]
    query_columns = w_out.shape[0]
    key_value_columns = (channels - query_columns) // 2
    req_count = lax.axis_size("req")
    rep_count = lax.axis_size("rep")
    rep_index = lax.axis_index("rep")
    requests = cache_len.shape[0]
    owner_page_count = requests // rep_count
    tree_length = parents.shape[1]
    own_start = rep_index * owner_page_count
    page_length = cache.shape[2]
    slots_count = page_table.shape[2]

    local_rows = hidden.reshape(owner_page_count, req_count, model_width)
    own_hidden = lax.all_to_all(local_rows, "req", split_axis=1, concat_axis=1, tiled=True)
    all_hidden = lax.all_gather(own_hidden, "rep", axis=0, tiled=True)

    normed = rms_scaled(all_hidden.astype(jnp.float32), norm_gain)
    projected = jnp.dot(
        normed.reshape(-1, model_width), w_qkv, preferred_element_type=jnp.float32
    ).astype(jnp.bfloat16).reshape(requests, tree_length, channels)

    reached = ancestors(parents)
    depths = jnp.sum(reached, axis=-1).astype(jnp.int32) - 1
    token_positions = cache_len[:, None] + depths
    flat_positions = token_positions.reshape(-1)
    head_columns = query_columns // QUERY_HEADS
    flat = projected.reshape(requests * tree_length, channels)
    queries = rotate_flat(
        flat[:, :query_columns].astype(jnp.float32), flat_positions, head_columns
    ).astype(jnp.bfloat16).reshape(requests, tree_length, query_columns)
    keys_all = rotate_flat(
        flat[:, query_columns : query_columns + key_value_columns].astype(jnp.float32),
        flat_positions,
        head_columns,
    ).astype(jnp.bfloat16).reshape(requests, tree_length, key_value_columns)
    values_all = projected[..., query_columns + key_value_columns :]

    page_list = page_table[:, 0, :]
    starts = (
        jnp.arange(slots_count, dtype=jnp.int32)[None, :] * rep_count + rep_index
    ) * page_length
    limits = cache_len[:, None] - starts
    mine = (jnp.arange(requests, dtype=jnp.int32) // owner_page_count) == rep_index
    draft_mask = jnp.where(mine[:, None, None], reached, 0.0)
    sums, stats = paged_partials(
        queries, cache, page_list, limits, keys_all, values_all, draft_mask
    )
    peak_all = lax.pmax(stats[:, :, 0, :], "rep")
    joined = rescale(sums, stats, peak_all)
    shared = lax.psum_scatter(joined, "rep", scatter_dimension=0, tiled=True)
    attended = finish_attention(shared, owner_page_count, tree_length)

    mixed = jnp.dot(attended, w_out, preferred_element_type=jnp.float32)
    residual = (mixed + own_hidden.reshape(-1, model_width).astype(jnp.float32)).astype(
        jnp.bfloat16
    )
    residual_wide = residual.astype(jnp.float32)
    ffn_in = rms_scaled(residual_wide, ffn_gain).reshape(owner_page_count, tree_length, model_width)
    rows_in = lax.all_gather(ffn_in, "rep", axis=0, tiled=True).reshape(-1, model_width)
    gate = jnp.dot(rows_in, w_gate, preferred_element_type=jnp.float32)
    up = jnp.dot(rows_in, w_up, preferred_element_type=jnp.float32)
    activated = (jax.nn.silu(gate) * up).astype(jnp.bfloat16)
    ffn_sum = lax.psum_scatter(
        jnp.dot(activated, w_down, preferred_element_type=jnp.float32).reshape(
            requests, tree_length, model_width
        ),
        "rep",
        scatter_dimension=0,
        tiled=True,
    )
    out_own = (ffn_sum + residual_wide.reshape(owner_page_count, tree_length, model_width)).astype(
        jnp.bfloat16
    )
    out = lax.all_to_all(out_own, "req", split_axis=1, concat_axis=1, tiled=True)
    out = out.reshape(block_rows, draft_part, model_width)

    all_rows = path_rows(keys_all, values_all, reached, depths, accept_leaf)
    new_pages = place_rows(all_rows, page_slot, own_start, owner_page_count)
    return (out, new_pages)


def solution(mesh):
    placed = (
        P("rep", "req", None),
        P(),
        P(),
        P(),
        P(),
        P(None, "rep"),
        P(None, "rep"),
        P("rep", None),
        P(("req", "rep"), None, None, None),
        P("req", "rep", None),
        P("req"),
        P("req", None),
        P("req"),
        P("req"),
    )
    return jax.shard_map(
        body,
        mesh=mesh,
        in_specs=placed,
        out_specs=(P("rep", "req", None), P(("req", "rep"), None, None, None)),
        check_vma=False,
    )
```

```python
import functools

import jax
import jax.numpy as jnp
from jax import lax
from jax.experimental import pallas as pl
from jax.experimental.pallas import tpu as pltpu
from jax.sharding import PartitionSpec as P

QUERY_HEADS = 18
KEY_VALUE_HEADS = 6
ACC = 8


SCALE = 0.125
EPSILON = 1e-05
THETA = 10000.0


def apply_rotation(values, token_positions, head_count):
    head_columns = values.shape[-1] // head_count
    half_width = head_columns // 2
    shaped = values.reshape(values.shape[:-1] + (head_count, head_columns))
    frequency = THETA ** (-jnp.arange(half_width, dtype=jnp.float32) / half_width)
    angles = token_positions.astype(jnp.float32)[..., None] * frequency
    cosine = jnp.cos(angles)[..., None, :]
    sines = jnp.sin(angles)[..., None, :]
    front_half = shaped[..., :half_width]
    back_half = shaped[..., half_width:]
    turned = jnp.concatenate(
        [front_half * cosine - back_half * sines, back_half * cosine + front_half * sines], axis=-1
    )
    return turned.reshape(values.shape)


def ancestors(parents):
    tree_length = parents.shape[-1]
    identity = jnp.eye(tree_length, dtype=jnp.float32)
    linked = jax.nn.one_hot(parents, tree_length, dtype=jnp.float32)
    reached = jnp.minimum(identity + linked, 1.0)
    for doubling in range(tree_length.bit_length()):
        reached = jnp.minimum(
            jnp.einsum("rts,rsu->rtu", reached, reached, precision=lax.Precision.HIGHEST), 1.0
        )
    return reached


def rms_scaled(values_in, gain):
    scaling = lax.rsqrt(jnp.mean(values_in * values_in, axis=-1, keepdims=True) + EPSILON)
    return (values_in * scaling * gain).astype(jnp.bfloat16)


def path_rows(key_matrix, value_matrix, reached, depths, leaf_ids):
    tree_length = reached.shape[-1]
    leaf_hot = jax.nn.one_hot(leaf_ids, tree_length, dtype=jnp.float32)
    on_path = jnp.einsum("rt,rts->rs", leaf_hot, reached, precision=lax.Precision.HIGHEST)
    level_hot = (depths[:, None, :] == jnp.arange(ACC, dtype=jnp.int32)[None, :, None]).astype(
        jnp.float32
    )
    selector = (on_path[:, None, :] * level_hot).astype(jnp.bfloat16)
    stacked = jnp.stack([key_matrix, value_matrix], axis=1)
    return jnp.einsum(
        "ras,rbsc->rbac", selector, stacked, preferred_element_type=jnp.float32
    ).astype(jnp.bfloat16)


def place_rows(rows, page_slot, own_start, owner_page_count):
    slot_ids = own_start + jnp.arange(owner_page_count, dtype=jnp.int32)
    chooser = (page_slot[None, :] == slot_ids[:, None]).astype(jnp.bfloat16)
    return jnp.einsum("pr,rbac->pbac", chooser, rows, preferred_element_type=jnp.float32).astype(
        jnp.bfloat16
    )


def paged_kernel(slots, chunks, page_ref, limit_ref, *refs):
    q_ref = refs[0]
    page_refs = refs[1 : 1 + slots]
    dk_ref, dv_ref, dmask_ref = refs[1 + slots : 4 + slots]
    (part_ref,) = refs[4 + slots :]
    request = pl.program_id(0)
    tree_length = q_ref.shape[1]
    page_length = page_refs[0].shape[2]
    rows = 6 * tree_length
    half = rows // 2
    low_t = lax.broadcasted_iota(jnp.int32, (tree_length, 128), 1) < 64
    low_h = lax.broadcasted_iota(jnp.int32, (half, 128), 1) < 64
    key_lanes = lax.broadcasted_iota(jnp.int32, (rows, page_length), 1)
    stat_lanes = lax.broadcasted_iota(jnp.int32, (rows, 128), 1)
    draft_open = jnp.concatenate([dmask_ref[0]] * 6, axis=0) > 0.5
    nt = (((1,), (1,)), ((), ()))
    for c in range(chunks):
        lanes = pl.ds(c * 128, 128)
        tiles = [q_ref[0, :, pl.ds(c * 384 + 128 * j, 128)].astype(jnp.float32) for j in range(3)]
        turned0 = pltpu.roll(tiles[0], 64, 1)
        turned2 = pltpu.roll(tiles[2], 64, 1)
        blocks = [
            jnp.where(low_t, tiles[0], 0.0),
            jnp.where(low_t, turned0, 0.0),
            jnp.where(low_t, tiles[1], 0.0),
            jnp.where(low_t, 0.0, tiles[1]),
            jnp.where(low_t, 0.0, turned2),
            jnp.where(low_t, 0.0, tiles[2]),
        ]
        qc = jnp.concatenate(blocks, axis=0).astype(jnp.bfloat16)
        parts = []
        for s in range(slots):
            kc = page_refs[s][0, 0, :, lanes]
            sc = lax.dot_general(qc, kc, nt, preferred_element_type=jnp.float32) * SCALE
            sc = jnp.where(key_lanes < limit_ref[request, s], sc, -jnp.inf)
            parts.append(sc)
        kd = dk_ref[0, :, lanes]
        sd = lax.dot_general(qc, kd, nt, preferred_element_type=jnp.float32) * SCALE
        sd = jnp.where(draft_open, sd, -jnp.inf)
        peak = jnp.max(sd, axis=-1, keepdims=True)
        for sc in parts:
            peak = jnp.maximum(peak, jnp.max(sc, axis=-1, keepdims=True))
        wd = jnp.exp(sd - peak)
        total = jnp.sum(wd, axis=-1, keepdims=True)
        acc = jnp.dot(
            wd.astype(jnp.bfloat16), dv_ref[0, :, lanes], preferred_element_type=jnp.float32
        )
        for s in range(slots):
            ws = jnp.exp(parts[s] - peak)
            total = total + jnp.sum(ws, axis=-1, keepdims=True)
            acc = acc + jnp.dot(
                ws.astype(jnp.bfloat16),
                page_refs[s][0, 1, :, lanes],
                preferred_element_type=jnp.float32,
            )
        part_ref[0, c, 0:half, :] = jnp.where(low_h, acc[:half], acc[half:])
        stats = jnp.where(stat_lanes == 0, total, jnp.where(stat_lanes == 1, peak, 0.0))
        flipped = jnp.transpose(stats)
        pieces = [flipped[j : j + 1, 128 * p : 128 * (p + 1)] for j in range(2) for p in range(3)]
        pieces.append(jnp.zeros((2, 128), jnp.float32))
        part_ref[0, c, half : half + 8, :] = jnp.concatenate(pieces, axis=0)


def paged_partials(queries, cache, page_list, limits, draft_keys, draft_values, draft_mask):
    requests, tree_length, query_columns = queries.shape
    chunks = KEY_VALUE_HEADS // 2
    rows = 6 * tree_length
    slots = page_list.shape[1]
    page_length = cache.shape[2]
    width = cache.shape[3]

    def page_map(s):
        return lambda k, pages, limit: (pages[k, s], 0, 0, 0)

    in_specs = [pl.BlockSpec((1, tree_length, query_columns), lambda k, pages, limit: (k, 0, 0))]
    in_specs += [pl.BlockSpec((1, 2, page_length, width), page_map(s)) for s in range(slots)]
    in_specs += [
        pl.BlockSpec((1, tree_length, width), lambda k, pages, limit: (k, 0, 0)),
        pl.BlockSpec((1, tree_length, width), lambda k, pages, limit: (k, 0, 0)),
        pl.BlockSpec((1, tree_length, tree_length), lambda k, pages, limit: (k, 0, 0)),
    ]
    out_specs = [
        pl.BlockSpec((1, chunks, rows // 2 + 8, 128), lambda k, pages, limit: (k, 0, 0, 0)),
    ]
    out_shape = [
        jax.ShapeDtypeStruct((requests, chunks, rows // 2 + 8, 128), jnp.float32),
    ]
    keys_seen = slots * page_length + tree_length
    cost = pl.CostEstimate(
        flops=requests * chunks * rows * 128 * keys_seen * 4,
        bytes_accessed=requests * (slots * 2 * page_length * width * 2 + chunks * rows * 128 * 3),
        transcendentals=requests * chunks * rows * keys_seen,
    )
    grid_spec = pltpu.PrefetchScalarGridSpec(
        num_scalar_prefetch=2,
        grid=(requests,),
        in_specs=in_specs,
        out_specs=out_specs,
    )
    return pl.pallas_call(
        functools.partial(paged_kernel, slots, chunks),
        grid_spec=grid_spec,
        out_shape=out_shape,
        cost_estimate=cost,
        compiler_params=pltpu.CompilerParams(dimension_semantics=("arbitrary",)),
        name="paged_partials",
    )(page_list, limits, queries, *([cache] * slots), draft_keys, draft_values, draft_mask)


def combine_kernel(part_ref, out_ref):
    holders, chunks = part_ref.shape[0], part_ref.shape[2]
    half = out_ref.shape[2]
    rows = 2 * half
    pieces = rows // 128
    low_h = lax.broadcasted_iota(jnp.int32, (half, 128), 1) < 64

    def as_column(row):
        column = jnp.transpose(jnp.broadcast_to(row, (128, rows)))
        return jnp.where(low_h, column[:half], column[half:])

    for c in range(chunks):
        tails = [part_ref[h, 0, c, half : half + 8, :] for h in range(holders)]
        totals = [jnp.concatenate([t[p : p + 1] for p in range(pieces)], axis=1) for t in tails]
        peaks = [
            jnp.concatenate([t[pieces + p : pieces + p + 1] for p in range(pieces)], axis=1)
            for t in tails
        ]
        top = peaks[0]
        for peak in peaks[1:]:
            top = jnp.maximum(top, peak)
        total = jnp.zeros_like(top)
        acc = jnp.zeros((half, 128), jnp.float32)
        for h in range(holders):
            factor = jnp.exp(peaks[h] - top)
            total = total + totals[h] * factor
            acc = acc + part_ref[h, 0, c, 0:half, :] * as_column(factor)
        out_ref[0, c] = (acc / as_column(total)).astype(out_ref.dtype)


def combine(parts):
    holders, requests, chunks, rows_in, lanes = parts.shape
    half = rows_in - 8
    return pl.pallas_call(
        combine_kernel,
        grid=(requests,),
        in_specs=[pl.BlockSpec((holders, 1, chunks, rows_in, lanes), lambda k: (0, k, 0, 0, 0))],
        out_specs=pl.BlockSpec((1, chunks, half, lanes), lambda k: (k, 0, 0, 0)),
        out_shape=jax.ShapeDtypeStruct((requests, chunks, half, lanes), jnp.bfloat16),
        compiler_params=pltpu.CompilerParams(dimension_semantics=("arbitrary",)),
        name="combine_holders",
    )(parts)


def finish_attention(attended, requests, tree_length):
    group = QUERY_HEADS // KEY_VALUE_HEADS
    chunks = attended.shape[1]
    shaped = attended.reshape(requests, chunks, group, tree_length, 2, 64)
    result = shaped.transpose(0, 3, 1, 4, 2, 5)
    return result.reshape(requests * tree_length, chunks * 2 * group * 64)


def rotate_flat(values, token_positions, head_columns):
    half_width = head_columns // 2
    frequency = THETA ** (-jnp.arange(half_width, dtype=jnp.float32) / half_width)
    angles = token_positions.astype(jnp.float32)[:, None] * frequency
    cosine = jnp.cos(angles)
    sines = jnp.sin(angles)
    repeats = values.shape[-1] // head_columns
    cosine = jnp.tile(jnp.concatenate([cosine, cosine], axis=-1), (1, repeats))
    sines = jnp.tile(jnp.concatenate([-sines, sines], axis=-1), (1, repeats))
    columns = jnp.arange(values.shape[-1], dtype=jnp.int32)
    front = (columns % head_columns) < half_width
    partner = jnp.where(
        front[None, :], jnp.roll(values, -half_width, axis=-1), jnp.roll(values, half_width, axis=-1)
    )
    return values * cosine + partner * sines


def body(
    hidden,
    norm_gain,
    w_qkv,
    w_out,
    ffn_gain,
    w_gate,
    w_up,
    w_down,
    cache,
    page_table,
    cache_len,
    parents,
    accept_leaf,
    page_slot,
):
    block_rows, draft_part, model_width = hidden.shape
    channels = w_qkv.shape[1]
    query_columns = w_out.shape[0]
    key_value_columns = (channels - query_columns) // 2
    req_count = lax.axis_size("req")
    rep_count = lax.axis_size("rep")
    rep_index = lax.axis_index("rep")
    requests = cache_len.shape[0]
    owner_page_count = requests // rep_count
    tree_length = parents.shape[1]
    own_start = rep_index * owner_page_count
    page_length = cache.shape[2]
    slots_count = page_table.shape[2]

    local_rows = hidden.reshape(owner_page_count, req_count, model_width)
    own_hidden = lax.all_to_all(local_rows, "req", split_axis=1, concat_axis=1, tiled=True)
    all_hidden = lax.all_gather(own_hidden, "rep", axis=0, tiled=True)

    normed = rms_scaled(all_hidden.astype(jnp.float32), norm_gain)
    projected = jnp.dot(
        normed.reshape(-1, model_width), w_qkv, preferred_element_type=jnp.float32
    ).astype(jnp.bfloat16).reshape(requests, tree_length, channels)

    reached = ancestors(parents)
    depths = jnp.sum(reached, axis=-1).astype(jnp.int32) - 1
    token_positions = cache_len[:, None] + depths
    flat_positions = token_positions.reshape(-1)
    head_columns = query_columns // QUERY_HEADS
    flat = projected.reshape(requests * tree_length, channels)
    queries = rotate_flat(
        flat[:, :query_columns].astype(jnp.float32), flat_positions, head_columns
    ).astype(jnp.bfloat16).reshape(requests, tree_length, query_columns)
    keys_all = rotate_flat(
        flat[:, query_columns : query_columns + key_value_columns].astype(jnp.float32),
        flat_positions,
        head_columns,
    ).astype(jnp.bfloat16).reshape(requests, tree_length, key_value_columns)
    values_all = projected[..., query_columns + key_value_columns :]

    page_list = page_table[:, 0, :]
    starts = (
        jnp.arange(slots_count, dtype=jnp.int32)[None, :] * rep_count + rep_index
    ) * page_length
    limits = cache_len[:, None] - starts
    mine = (jnp.arange(requests, dtype=jnp.int32) // owner_page_count) == rep_index
    draft_mask = jnp.where(mine[:, None, None], reached, 0.0)
    (parts,) = paged_partials(
        queries, cache, page_list, limits, keys_all, values_all, draft_mask
    )
    parts = parts.reshape((rep_count, owner_page_count) + parts.shape[1:])
    gathered = lax.all_to_all(parts, "rep", split_axis=0, concat_axis=0, tiled=True)
    attended = finish_attention(combine(gathered), owner_page_count, tree_length)

    mixed = jnp.dot(attended, w_out, preferred_element_type=jnp.float32)
    residual = (mixed + own_hidden.reshape(-1, model_width).astype(jnp.float32)).astype(
        jnp.bfloat16
    )
    residual_wide = residual.astype(jnp.float32)
    ffn_in = rms_scaled(residual_wide, ffn_gain).reshape(owner_page_count, tree_length, model_width)
    rows_in = lax.all_gather(ffn_in, "rep", axis=0, tiled=True).reshape(-1, model_width)
    gate = jnp.dot(rows_in, w_gate, preferred_element_type=jnp.float32)
    up = jnp.dot(rows_in, w_up, preferred_element_type=jnp.float32)
    activated = (jax.nn.silu(gate) * up).astype(jnp.bfloat16)
    ffn_sum = lax.psum_scatter(
        jnp.dot(activated, w_down, preferred_element_type=jnp.float32).reshape(
            requests, tree_length, model_width
        ),
        "rep",
        scatter_dimension=0,
        tiled=True,
    )
    out_own = (ffn_sum + residual_wide.reshape(owner_page_count, tree_length, model_width)).astype(
        jnp.bfloat16
    )
    out = lax.all_to_all(out_own, "req", split_axis=1, concat_axis=1, tiled=True)
    out = out.reshape(block_rows, draft_part, model_width)

    all_rows = path_rows(keys_all, values_all, reached, depths, accept_leaf)
    new_pages = place_rows(all_rows, page_slot, own_start, owner_page_count)
    return (out, new_pages)


def solution(mesh):
    placed = (
        P("rep", "req", None),
        P(),
        P(),
        P(),
        P(),
        P(None, "rep"),
        P(None, "rep"),
        P("rep", None),
        P(("req", "rep"), None, None, None),
        P("req", "rep", None),
        P("req"),
        P("req", None),
        P("req"),
        P("req"),
    )
    return jax.shard_map(
        body,
        mesh=mesh,
        in_specs=placed,
        out_specs=(P("rep", "req", None), P(("req", "rep"), None, None, None)),
        check_vma=False,
    )
```

```python
import functools

import jax
import jax.numpy as jnp
from jax import lax
from jax.experimental import pallas as pl
from jax.experimental.pallas import tpu as pltpu
from jax.sharding import PartitionSpec as P

QUERY_HEADS = 18
KEY_VALUE_HEADS = 6
ACC = 8


SCALE = 0.125
EPSILON = 1e-05
THETA = 10000.0


def apply_rotation(values, token_positions, head_count):
    head_columns = values.shape[-1] // head_count
    half_width = head_columns // 2
    shaped = values.reshape(values.shape[:-1] + (head_count, head_columns))
    frequency = THETA ** (-jnp.arange(half_width, dtype=jnp.float32) / half_width)
    angles = token_positions.astype(jnp.float32)[..., None] * frequency
    cosine = jnp.cos(angles)[..., None, :]
    sines = jnp.sin(angles)[..., None, :]
    front_half = shaped[..., :half_width]
    back_half = shaped[..., half_width:]
    turned = jnp.concatenate(
        [front_half * cosine - back_half * sines, back_half * cosine + front_half * sines], axis=-1
    )
    return turned.reshape(values.shape)


def ancestors(parents):
    tree_length = parents.shape[-1]
    identity = jnp.eye(tree_length, dtype=jnp.float32)
    linked = jax.nn.one_hot(parents, tree_length, dtype=jnp.float32)
    reached = jnp.minimum(identity + linked, 1.0)
    for doubling in range(tree_length.bit_length()):
        reached = jnp.minimum(
            jnp.einsum("rts,rsu->rtu", reached, reached, precision=lax.Precision.HIGHEST), 1.0
        )
    return reached


def rms_scaled(values_in, gain):
    scaling = lax.rsqrt(jnp.mean(values_in * values_in, axis=-1, keepdims=True) + EPSILON)
    return (values_in * scaling * gain).astype(jnp.bfloat16)


def path_rows(key_matrix, value_matrix, reached, depths, leaf_ids):
    tree_length = reached.shape[-1]
    leaf_hot = jax.nn.one_hot(leaf_ids, tree_length, dtype=jnp.float32)
    on_path = jnp.einsum("rt,rts->rs", leaf_hot, reached, precision=lax.Precision.HIGHEST)
    level_hot = (depths[:, None, :] == jnp.arange(ACC, dtype=jnp.int32)[None, :, None]).astype(
        jnp.float32
    )
    selector = (on_path[:, None, :] * level_hot).astype(jnp.bfloat16)
    stacked = jnp.stack([key_matrix, value_matrix], axis=1)
    return jnp.einsum(
        "ras,rbsc->rbac", selector, stacked, preferred_element_type=jnp.float32
    ).astype(jnp.bfloat16)


def place_rows(rows, page_slot, own_start, owner_page_count):
    slot_ids = own_start + jnp.arange(owner_page_count, dtype=jnp.int32)
    chooser = (page_slot[None, :] == slot_ids[:, None]).astype(jnp.bfloat16)
    return jnp.einsum("pr,rbac->pbac", chooser, rows, preferred_element_type=jnp.float32).astype(
        jnp.bfloat16
    )


def paged_kernel(slots, chunks, page_ref, limit_ref, *refs):
    q_ref = refs[0]
    page_refs = refs[1 : 1 + slots]
    dk_ref, dv_ref, dmask_ref = refs[1 + slots : 4 + slots]
    (part_ref,) = refs[4 + slots :]
    request = pl.program_id(0)
    tree_length = q_ref.shape[1]
    page_length = page_refs[0].shape[2]
    rows = 6 * tree_length
    half = rows // 2
    low_t = lax.broadcasted_iota(jnp.int32, (tree_length, 128), 1) < 64
    low_h = lax.broadcasted_iota(jnp.int32, (half, 128), 1) < 64
    key_lanes = lax.broadcasted_iota(jnp.int32, (rows, page_length), 1)
    stat_lanes = lax.broadcasted_iota(jnp.int32, (rows, 128), 1)
    draft_open = jnp.concatenate([dmask_ref[0]] * 6, axis=0) > 0.5
    nt = (((1,), (1,)), ((), ()))
    for c in range(chunks):
        lanes = pl.ds(c * 128, 128)
        tiles = [q_ref[0, :, pl.ds(c * 384 + 128 * j, 128)].astype(jnp.float32) for j in range(3)]
        turned0 = pltpu.roll(tiles[0], 64, 1)
        turned2 = pltpu.roll(tiles[2], 64, 1)
        blocks = [
            jnp.where(low_t, tiles[0], 0.0),
            jnp.where(low_t, turned0, 0.0),
            jnp.where(low_t, tiles[1], 0.0),
            jnp.where(low_t, 0.0, tiles[1]),
            jnp.where(low_t, 0.0, turned2),
            jnp.where(low_t, 0.0, tiles[2]),
        ]
        qc = jnp.concatenate(blocks, axis=0).astype(jnp.bfloat16)
        parts = []
        for s in range(slots):
            kc = page_refs[s][0, 0, :, lanes]
            sc = lax.dot_general(qc, kc, nt, preferred_element_type=jnp.float32) * SCALE
            sc = jnp.where(key_lanes < limit_ref[request, s], sc, -jnp.inf)
            parts.append(sc)
        kd = dk_ref[0, :, lanes]
        sd = lax.dot_general(qc, kd, nt, preferred_element_type=jnp.float32) * SCALE
        sd = jnp.where(draft_open, sd, -jnp.inf)
        peak = jnp.max(sd, axis=-1, keepdims=True)
        for sc in parts:
            peak = jnp.maximum(peak, jnp.max(sc, axis=-1, keepdims=True))
        wd = jnp.exp(sd - peak)
        total = jnp.sum(wd, axis=-1, keepdims=True)
        acc = jnp.dot(
            wd.astype(jnp.bfloat16), dv_ref[0, :, lanes], preferred_element_type=jnp.float32
        )
        for s in range(slots):
            ws = jnp.exp(parts[s] - peak)
            total = total + jnp.sum(ws, axis=-1, keepdims=True)
            acc = acc + jnp.dot(
                ws.astype(jnp.bfloat16),
                page_refs[s][0, 1, :, lanes],
                preferred_element_type=jnp.float32,
            )
        part_ref[0, c, 0:half, :] = jnp.where(low_h, acc[:half], acc[half:])
        stats = jnp.where(stat_lanes == 0, total, jnp.where(stat_lanes == 1, peak, 0.0))
        flipped = jnp.transpose(stats)
        pieces = [flipped[j : j + 1, 128 * p : 128 * (p + 1)] for j in range(2) for p in range(3)]
        pieces.append(jnp.zeros((2, 128), jnp.float32))
        part_ref[0, c, half : half + 8, :] = jnp.concatenate(pieces, axis=0)


def paged_partials(queries, cache, page_list, limits, draft_keys, draft_values, draft_mask):
    requests, tree_length, query_columns = queries.shape
    chunks = KEY_VALUE_HEADS // 2
    rows = 6 * tree_length
    slots = page_list.shape[1]
    page_length = cache.shape[2]
    width = cache.shape[3]

    def page_map(s):
        return lambda k, pages, limit: (pages[k, s], 0, 0, 0)

    in_specs = [pl.BlockSpec((1, tree_length, query_columns), lambda k, pages, limit: (k, 0, 0))]
    in_specs += [pl.BlockSpec((1, 2, page_length, width), page_map(s)) for s in range(slots)]
    in_specs += [
        pl.BlockSpec((1, tree_length, width), lambda k, pages, limit: (k, 0, 0)),
        pl.BlockSpec((1, tree_length, width), lambda k, pages, limit: (k, 0, 0)),
        pl.BlockSpec((1, tree_length, tree_length), lambda k, pages, limit: (k, 0, 0)),
    ]
    out_specs = [
        pl.BlockSpec((1, chunks, rows // 2 + 8, 128), lambda k, pages, limit: (k, 0, 0, 0)),
    ]
    out_shape = [
        jax.ShapeDtypeStruct((requests, chunks, rows // 2 + 8, 128), jnp.float32),
    ]
    keys_seen = slots * page_length + tree_length
    cost = pl.CostEstimate(
        flops=requests * chunks * rows * 128 * keys_seen * 4,
        bytes_accessed=requests * (slots * 2 * page_length * width * 2 + chunks * rows * 128 * 3),
        transcendentals=requests * chunks * rows * keys_seen,
    )
    grid_spec = pltpu.PrefetchScalarGridSpec(
        num_scalar_prefetch=2,
        grid=(requests,),
        in_specs=in_specs,
        out_specs=out_specs,
    )
    return pl.pallas_call(
        functools.partial(paged_kernel, slots, chunks),
        grid_spec=grid_spec,
        out_shape=out_shape,
        cost_estimate=cost,
        compiler_params=pltpu.CompilerParams(dimension_semantics=("arbitrary",)),
        name="paged_partials",
    )(page_list, limits, queries, *([cache] * slots), draft_keys, draft_values, draft_mask)


def exchange_kernel(count, same, x_ref, out_ref, local_sem, send_sems, recv_sems):
    me = lax.axis_index("rep")
    row = lax.axis_index("req")
    mesh_ids = pl.DeviceIdType.MESH
    barrier = pltpu.get_barrier_semaphore()
    for step in range(1, count):
        peer = lax.rem(me + step, count)
        pl.semaphore_signal(barrier, inc=1, device_id=(row, peer), device_id_type=mesh_ids)
    pl.semaphore_wait(barrier, count - 1)
    own = x_ref.at[0] if same else x_ref.at[me]
    local = pltpu.make_async_copy(own, out_ref.at[me], local_sem)
    local.start()
    sends = []
    for step in range(1, count):
        peer = lax.rem(me + step, count)
        source = x_ref.at[0] if same else x_ref.at[peer]
        copy = pltpu.make_async_remote_copy(
            src_ref=source,
            dst_ref=out_ref.at[me],
            send_sem=send_sems.at[step],
            recv_sem=recv_sems.at[step],
            device_id=(row, peer),
            device_id_type=mesh_ids,
        )
        copy.start()
        sends.append(copy)
    local.wait()
    for copy in sends:
        copy.wait_send()
    for step in range(1, count):
        origin = lax.rem(me + count - step, count)
        incoming = pltpu.make_async_remote_copy(
            src_ref=x_ref.at[0],
            dst_ref=out_ref.at[origin],
            send_sem=send_sems.at[step],
            recv_sem=recv_sems.at[step],
            device_id=(row, origin),
            device_id_type=mesh_ids,
        )
        incoming.wait_recv()


def exchange(blocks, count, same, collective_id):
    out_shape = jax.ShapeDtypeStruct((count,) + blocks.shape[1:], blocks.dtype)
    moved = blocks[0].size * blocks.dtype.itemsize * (count - 1)
    return pl.pallas_call(
        functools.partial(exchange_kernel, count, same),
        in_specs=[pl.BlockSpec(memory_space=pl.ANY)],
        out_specs=pl.BlockSpec(memory_space=pl.ANY),
        out_shape=out_shape,
        scratch_shapes=[
            pltpu.SemaphoreType.DMA(()),
            pltpu.SemaphoreType.DMA((count,)),
            pltpu.SemaphoreType.DMA((count,)),
        ],
        compiler_params=pltpu.CompilerParams(collective_id=collective_id, has_side_effects=True),
        cost_estimate=pl.CostEstimate(flops=0, bytes_accessed=2 * moved, transcendentals=0),
        name=f"exchange_{collective_id}",
    )(blocks)


def combine_kernel(part_ref, out_ref):
    holders, chunks = part_ref.shape[0], part_ref.shape[2]
    half = out_ref.shape[2]
    rows = 2 * half
    pieces = rows // 128
    low_h = lax.broadcasted_iota(jnp.int32, (half, 128), 1) < 64

    def as_column(row):
        column = jnp.transpose(jnp.broadcast_to(row, (128, rows)))
        return jnp.where(low_h, column[:half], column[half:])

    for c in range(chunks):
        tails = [part_ref[h, 0, c, half : half + 8, :] for h in range(holders)]
        totals = [jnp.concatenate([t[p : p + 1] for p in range(pieces)], axis=1) for t in tails]
        peaks = [
            jnp.concatenate([t[pieces + p : pieces + p + 1] for p in range(pieces)], axis=1)
            for t in tails
        ]
        top = peaks[0]
        for peak in peaks[1:]:
            top = jnp.maximum(top, peak)
        total = jnp.zeros_like(top)
        acc = jnp.zeros((half, 128), jnp.float32)
        for h in range(holders):
            factor = jnp.exp(peaks[h] - top)
            total = total + totals[h] * factor
            acc = acc + part_ref[h, 0, c, 0:half, :] * as_column(factor)
        out_ref[0, c] = (acc / as_column(total)).astype(out_ref.dtype)


def combine(parts):
    holders, requests, chunks, rows_in, lanes = parts.shape
    half = rows_in - 8
    return pl.pallas_call(
        combine_kernel,
        grid=(requests,),
        in_specs=[pl.BlockSpec((holders, 1, chunks, rows_in, lanes), lambda k: (0, k, 0, 0, 0))],
        out_specs=pl.BlockSpec((1, chunks, half, lanes), lambda k: (k, 0, 0, 0)),
        out_shape=jax.ShapeDtypeStruct((requests, chunks, half, lanes), jnp.bfloat16),
        compiler_params=pltpu.CompilerParams(dimension_semantics=("arbitrary",)),
        name="combine_holders",
    )(parts)


def finish_attention(attended, requests, tree_length):
    group = QUERY_HEADS // KEY_VALUE_HEADS
    chunks = attended.shape[1]
    shaped = attended.reshape(requests, chunks, group, tree_length, 2, 64)
    result = shaped.transpose(0, 3, 1, 4, 2, 5)
    return result.reshape(requests * tree_length, chunks * 2 * group * 64)


def rotate_flat(values, token_positions, head_columns):
    half_width = head_columns // 2
    frequency = THETA ** (-jnp.arange(half_width, dtype=jnp.float32) / half_width)
    angles = token_positions.astype(jnp.float32)[:, None] * frequency
    cosine = jnp.cos(angles)
    sines = jnp.sin(angles)
    repeats = values.shape[-1] // head_columns
    cosine = jnp.tile(jnp.concatenate([cosine, cosine], axis=-1), (1, repeats))
    sines = jnp.tile(jnp.concatenate([-sines, sines], axis=-1), (1, repeats))
    columns = jnp.arange(values.shape[-1], dtype=jnp.int32)
    front = (columns % head_columns) < half_width
    partner = jnp.where(
        front[None, :], jnp.roll(values, -half_width, axis=-1), jnp.roll(values, half_width, axis=-1)
    )
    return values * cosine + partner * sines


def body(
    hidden,
    norm_gain,
    w_qkv,
    w_out,
    ffn_gain,
    w_gate,
    w_up,
    w_down,
    cache,
    page_table,
    cache_len,
    parents,
    accept_leaf,
    page_slot,
):
    block_rows, draft_part, model_width = hidden.shape
    channels = w_qkv.shape[1]
    query_columns = w_out.shape[0]
    key_value_columns = (channels - query_columns) // 2
    req_count = lax.axis_size("req")
    rep_count = lax.axis_size("rep")
    rep_index = lax.axis_index("rep")
    requests = cache_len.shape[0]
    owner_page_count = requests // rep_count
    tree_length = parents.shape[1]
    own_start = rep_index * owner_page_count
    page_length = cache.shape[2]
    slots_count = page_table.shape[2]

    local_rows = hidden.reshape(owner_page_count, req_count, model_width)
    own_hidden = lax.all_to_all(local_rows, "req", split_axis=1, concat_axis=1, tiled=True)
    all_hidden = lax.all_gather(own_hidden, "rep", axis=0, tiled=True)

    normed = rms_scaled(all_hidden.astype(jnp.float32), norm_gain)
    projected = jnp.dot(
        normed.reshape(-1, model_width), w_qkv, preferred_element_type=jnp.float32
    ).astype(jnp.bfloat16).reshape(requests, tree_length, channels)

    reached = ancestors(parents)
    depths = jnp.sum(reached, axis=-1).astype(jnp.int32) - 1
    token_positions = cache_len[:, None] + depths
    flat_positions = token_positions.reshape(-1)
    head_columns = query_columns // QUERY_HEADS
    flat = projected.reshape(requests * tree_length, channels)
    queries = rotate_flat(
        flat[:, :query_columns].astype(jnp.float32), flat_positions, head_columns
    ).astype(jnp.bfloat16).reshape(requests, tree_length, query_columns)
    keys_all = rotate_flat(
        flat[:, query_columns : query_columns + key_value_columns].astype(jnp.float32),
        flat_positions,
        head_columns,
    ).astype(jnp.bfloat16).reshape(requests, tree_length, key_value_columns)
    values_all = projected[..., query_columns + key_value_columns :]

    page_list = page_table[:, 0, :]
    starts = (
        jnp.arange(slots_count, dtype=jnp.int32)[None, :] * rep_count + rep_index
    ) * page_length
    limits = cache_len[:, None] - starts
    mine = (jnp.arange(requests, dtype=jnp.int32) // owner_page_count) == rep_index
    draft_mask = jnp.where(mine[:, None, None], reached, 0.0)
    (parts,) = paged_partials(
        queries, cache, page_list, limits, keys_all, values_all, draft_mask
    )
    parts = parts.reshape((rep_count, owner_page_count) + parts.shape[1:])
    gathered = exchange(parts, rep_count, False, 1)
    attended = finish_attention(combine(gathered), owner_page_count, tree_length)

    mixed = jnp.dot(attended, w_out, preferred_element_type=jnp.float32)
    residual = (mixed + own_hidden.reshape(-1, model_width).astype(jnp.float32)).astype(
        jnp.bfloat16
    )
    residual_wide = residual.astype(jnp.float32)
    ffn_in = rms_scaled(residual_wide, ffn_gain).reshape(owner_page_count, tree_length, model_width)
    rows_in = exchange(ffn_in[None], rep_count, True, 2).reshape(-1, model_width)
    gate = jnp.dot(rows_in, w_gate, preferred_element_type=jnp.float32)
    up = jnp.dot(rows_in, w_up, preferred_element_type=jnp.float32)
    activated = (jax.nn.silu(gate) * up).astype(jnp.bfloat16)
    down = jnp.dot(activated, w_down, preferred_element_type=jnp.float32).reshape(
        rep_count, owner_page_count, tree_length, model_width
    )
    ffn_terms = exchange(down, rep_count, False, 3)
    out_own = (
        jnp.sum(ffn_terms, axis=0)
        + residual_wide.reshape(owner_page_count, tree_length, model_width)
    ).astype(jnp.bfloat16)
    out = lax.all_to_all(out_own, "req", split_axis=1, concat_axis=1, tiled=True)
    out = out.reshape(block_rows, draft_part, model_width)

    all_rows = path_rows(keys_all, values_all, reached, depths, accept_leaf)
    new_pages = place_rows(all_rows, page_slot, own_start, owner_page_count)
    return (out, new_pages)


def solution(mesh):
    placed = (
        P("rep", "req", None),
        P(),
        P(),
        P(),
        P(),
        P(None, "rep"),
        P(None, "rep"),
        P("rep", None),
        P(("req", "rep"), None, None, None),
        P("req", "rep", None),
        P("req"),
        P("req", None),
        P("req"),
        P("req"),
    )
    return jax.shard_map(
        body,
        mesh=mesh,
        in_specs=placed,
        out_specs=(P("rep", "req", None), P(("req", "rep"), None, None, None)),
        check_vma=False,
    )
```

```python
import functools

import jax
import jax.numpy as jnp
from jax import lax
from jax.experimental import pallas as pl
from jax.experimental.pallas import tpu as pltpu
from jax.sharding import PartitionSpec as P

QUERY_HEADS = 18
KEY_VALUE_HEADS = 6
ACC = 8


SCALE = 0.125
EPSILON = 1e-05
THETA = 10000.0


def apply_rotation(values, token_positions, head_count):
    head_columns = values.shape[-1] // head_count
    half_width = head_columns // 2
    shaped = values.reshape(values.shape[:-1] + (head_count, head_columns))
    frequency = THETA ** (-jnp.arange(half_width, dtype=jnp.float32) / half_width)
    angles = token_positions.astype(jnp.float32)[..., None] * frequency
    cosine = jnp.cos(angles)[..., None, :]
    sines = jnp.sin(angles)[..., None, :]
    front_half = shaped[..., :half_width]
    back_half = shaped[..., half_width:]
    turned = jnp.concatenate(
        [front_half * cosine - back_half * sines, back_half * cosine + front_half * sines], axis=-1
    )
    return turned.reshape(values.shape)


def ancestors(parents):
    tree_length = parents.shape[-1]
    identity = jnp.eye(tree_length, dtype=jnp.float32)
    linked = jax.nn.one_hot(parents, tree_length, dtype=jnp.float32)
    reached = jnp.minimum(identity + linked, 1.0)
    for doubling in range(tree_length.bit_length()):
        reached = jnp.minimum(
            jnp.einsum("rts,rsu->rtu", reached, reached, precision=lax.Precision.HIGHEST), 1.0
        )
    return reached


def rms_scaled(values_in, gain):
    scaling = lax.rsqrt(jnp.mean(values_in * values_in, axis=-1, keepdims=True) + EPSILON)
    return (values_in * scaling * gain).astype(jnp.bfloat16)


def path_rows(key_matrix, value_matrix, reached, depths, leaf_ids):
    tree_length = reached.shape[-1]
    leaf_hot = jax.nn.one_hot(leaf_ids, tree_length, dtype=jnp.float32)
    on_path = jnp.einsum("rt,rts->rs", leaf_hot, reached, precision=lax.Precision.HIGHEST)
    level_hot = (depths[:, None, :] == jnp.arange(ACC, dtype=jnp.int32)[None, :, None]).astype(
        jnp.float32
    )
    selector = (on_path[:, None, :] * level_hot).astype(jnp.bfloat16)
    stacked = jnp.stack([key_matrix, value_matrix], axis=1)
    return jnp.einsum(
        "ras,rbsc->rbac", selector, stacked, preferred_element_type=jnp.float32
    ).astype(jnp.bfloat16)


def place_rows(rows, page_slot, own_start, owner_page_count):
    slot_ids = own_start + jnp.arange(owner_page_count, dtype=jnp.int32)
    chooser = (page_slot[None, :] == slot_ids[:, None]).astype(jnp.bfloat16)
    return jnp.einsum("pr,rbac->pbac", chooser, rows, preferred_element_type=jnp.float32).astype(
        jnp.bfloat16
    )


def paged_kernel(slots, chunks, page_ref, limit_ref, *refs):
    q_ref = refs[0]
    page_refs = refs[1 : 1 + slots]
    dk_ref, dv_ref, dmask_ref = refs[1 + slots : 4 + slots]
    (part_ref,) = refs[4 + slots :]
    request = pl.program_id(0)
    tree_length = q_ref.shape[1]
    page_length = page_refs[0].shape[2]
    rows = 6 * tree_length
    half = rows // 2
    low_t = lax.broadcasted_iota(jnp.int32, (tree_length, 128), 1) < 64
    low_h = lax.broadcasted_iota(jnp.int32, (half, 128), 1) < 64
    key_lanes = lax.broadcasted_iota(jnp.int32, (rows, page_length), 1)
    stat_lanes = lax.broadcasted_iota(jnp.int32, (rows, 128), 1)
    draft_open = jnp.concatenate([dmask_ref[0]] * 6, axis=0) > 0.5
    nt = (((1,), (1,)), ((), ()))
    for c in range(chunks):
        lanes = pl.ds(c * 128, 128)
        tiles = [q_ref[0, :, pl.ds(c * 384 + 128 * j, 128)].astype(jnp.float32) for j in range(3)]
        turned0 = pltpu.roll(tiles[0], 64, 1)
        turned2 = pltpu.roll(tiles[2], 64, 1)
        blocks = [
            jnp.where(low_t, tiles[0], 0.0),
            jnp.where(low_t, turned0, 0.0),
            jnp.where(low_t, tiles[1], 0.0),
            jnp.where(low_t, 0.0, tiles[1]),
            jnp.where(low_t, 0.0, turned2),
            jnp.where(low_t, 0.0, tiles[2]),
        ]
        qc = jnp.concatenate(blocks, axis=0).astype(jnp.bfloat16)
        parts = []
        for s in range(slots):
            kc = page_refs[s][0, 0, :, lanes]
            sc = lax.dot_general(qc, kc, nt, preferred_element_type=jnp.float32) * SCALE
            sc = jnp.where(key_lanes < limit_ref[request, s], sc, -jnp.inf)
            parts.append(sc)
        kd = dk_ref[0, :, lanes]
        sd = lax.dot_general(qc, kd, nt, preferred_element_type=jnp.float32) * SCALE
        sd = jnp.where(draft_open, sd, -jnp.inf)
        peak = jnp.max(sd, axis=-1, keepdims=True)
        for sc in parts:
            peak = jnp.maximum(peak, jnp.max(sc, axis=-1, keepdims=True))
        peak_hi = peak.astype(jnp.bfloat16).astype(jnp.float32)
        peak_lo = (peak - peak_hi).astype(jnp.bfloat16).astype(jnp.float32)
        peak = peak_hi + peak_lo
        wd = jnp.exp(sd - peak)
        total = jnp.sum(wd, axis=-1, keepdims=True)
        acc = jnp.dot(
            wd.astype(jnp.bfloat16), dv_ref[0, :, lanes], preferred_element_type=jnp.float32
        )
        for s in range(slots):
            ws = jnp.exp(parts[s] - peak)
            total = total + jnp.sum(ws, axis=-1, keepdims=True)
            acc = acc + jnp.dot(
                ws.astype(jnp.bfloat16),
                page_refs[s][0, 1, :, lanes],
                preferred_element_type=jnp.float32,
            )
        part_ref[0, c, 0:half, :] = jnp.where(low_h, acc[:half], acc[half:]).astype(part_ref.dtype)
        stats = jnp.where(
            stat_lanes == 0,
            total,
            jnp.where(stat_lanes == 1, peak_hi, jnp.where(stat_lanes == 2, peak_lo, 0.0)),
        )
        flipped = jnp.transpose(stats)
        pieces = [flipped[j : j + 1, 128 * p : 128 * (p + 1)] for j in range(3) for p in range(3)]
        pieces.append(jnp.zeros((7, 128), jnp.float32))
        part_ref[0, c, half : half + 16, :] = jnp.concatenate(pieces, axis=0).astype(part_ref.dtype)


def paged_partials(queries, cache, page_list, limits, draft_keys, draft_values, draft_mask):
    requests, tree_length, query_columns = queries.shape
    chunks = KEY_VALUE_HEADS // 2
    rows = 6 * tree_length
    slots = page_list.shape[1]
    page_length = cache.shape[2]
    width = cache.shape[3]

    def page_map(s):
        return lambda k, pages, limit: (pages[k, s], 0, 0, 0)

    in_specs = [pl.BlockSpec((1, tree_length, query_columns), lambda k, pages, limit: (k, 0, 0))]
    in_specs += [pl.BlockSpec((1, 2, page_length, width), page_map(s)) for s in range(slots)]
    in_specs += [
        pl.BlockSpec((1, tree_length, width), lambda k, pages, limit: (k, 0, 0)),
        pl.BlockSpec((1, tree_length, width), lambda k, pages, limit: (k, 0, 0)),
        pl.BlockSpec((1, tree_length, tree_length), lambda k, pages, limit: (k, 0, 0)),
    ]
    out_specs = [
        pl.BlockSpec((1, chunks, rows // 2 + 16, 128), lambda k, pages, limit: (k, 0, 0, 0)),
    ]
    out_shape = [
        jax.ShapeDtypeStruct((requests, chunks, rows // 2 + 16, 128), jnp.bfloat16),
    ]
    keys_seen = slots * page_length + tree_length
    cost = pl.CostEstimate(
        flops=requests * chunks * rows * 128 * keys_seen * 4,
        bytes_accessed=requests * (slots * 2 * page_length * width * 2 + chunks * rows * 128 * 3),
        transcendentals=requests * chunks * rows * keys_seen,
    )
    grid_spec = pltpu.PrefetchScalarGridSpec(
        num_scalar_prefetch=2,
        grid=(requests,),
        in_specs=in_specs,
        out_specs=out_specs,
    )
    return pl.pallas_call(
        functools.partial(paged_kernel, slots, chunks),
        grid_spec=grid_spec,
        out_shape=out_shape,
        cost_estimate=cost,
        compiler_params=pltpu.CompilerParams(dimension_semantics=("arbitrary",)),
        name="paged_partials",
    )(page_list, limits, queries, *([cache] * slots), draft_keys, draft_values, draft_mask)


def exchange_kernel(count, same, x_ref, out_ref, local_sem, send_sems, recv_sems):
    me = lax.axis_index("rep")
    row = lax.axis_index("req")
    mesh_ids = pl.DeviceIdType.MESH
    barrier = pltpu.get_barrier_semaphore()
    for step in range(1, count):
        peer = lax.rem(me + step, count)
        pl.semaphore_signal(barrier, inc=1, device_id=(row, peer), device_id_type=mesh_ids)
    pl.semaphore_wait(barrier, count - 1)
    own = x_ref.at[0] if same else x_ref.at[me]
    local = pltpu.make_async_copy(own, out_ref.at[me], local_sem)
    local.start()
    sends = []
    for step in range(1, count):
        peer = lax.rem(me + step, count)
        source = x_ref.at[0] if same else x_ref.at[peer]
        copy = pltpu.make_async_remote_copy(
            src_ref=source,
            dst_ref=out_ref.at[me],
            send_sem=send_sems.at[step],
            recv_sem=recv_sems.at[step],
            device_id=(row, peer),
            device_id_type=mesh_ids,
        )
        copy.start()
        sends.append(copy)
    local.wait()
    for copy in sends:
        copy.wait_send()
    for step in range(1, count):
        origin = lax.rem(me + count - step, count)
        incoming = pltpu.make_async_remote_copy(
            src_ref=x_ref.at[0],
            dst_ref=out_ref.at[origin],
            send_sem=send_sems.at[step],
            recv_sem=recv_sems.at[step],
            device_id=(row, origin),
            device_id_type=mesh_ids,
        )
        incoming.wait_recv()


def exchange(blocks, count, same, collective_id):
    out_shape = jax.ShapeDtypeStruct((count,) + blocks.shape[1:], blocks.dtype)
    moved = blocks[0].size * blocks.dtype.itemsize * (count - 1)
    return pl.pallas_call(
        functools.partial(exchange_kernel, count, same),
        in_specs=[pl.BlockSpec(memory_space=pl.ANY)],
        out_specs=pl.BlockSpec(memory_space=pl.ANY),
        out_shape=out_shape,
        scratch_shapes=[
            pltpu.SemaphoreType.DMA(()),
            pltpu.SemaphoreType.DMA((count,)),
            pltpu.SemaphoreType.DMA((count,)),
        ],
        compiler_params=pltpu.CompilerParams(collective_id=collective_id, has_side_effects=True),
        cost_estimate=pl.CostEstimate(flops=0, bytes_accessed=2 * moved, transcendentals=0),
        name=f"exchange_{collective_id}",
    )(blocks)


def combine_kernel(part_ref, out_ref):
    holders, chunks = part_ref.shape[0], part_ref.shape[2]
    half = out_ref.shape[2]
    rows = 2 * half
    pieces = rows // 128
    low_h = lax.broadcasted_iota(jnp.int32, (half, 128), 1) < 64

    def as_column(row):
        column = jnp.transpose(jnp.broadcast_to(row, (128, rows)))
        return jnp.where(low_h, column[:half], column[half:])

    for c in range(chunks):
        tails = [
            part_ref[h, 0, c, half : half + 16, :].astype(jnp.float32) for h in range(holders)
        ]
        totals = [jnp.concatenate([t[p : p + 1] for p in range(pieces)], axis=1) for t in tails]
        peaks = [
            jnp.concatenate([t[pieces + p : pieces + p + 1] for p in range(pieces)], axis=1)
            + jnp.concatenate([t[2 * pieces + p : 2 * pieces + p + 1] for p in range(pieces)], axis=1)
            for t in tails
        ]
        top = peaks[0]
        for peak in peaks[1:]:
            top = jnp.maximum(top, peak)
        total = jnp.zeros_like(top)
        acc = jnp.zeros((half, 128), jnp.float32)
        for h in range(holders):
            factor = jnp.exp(peaks[h] - top)
            total = total + totals[h] * factor
            acc = acc + part_ref[h, 0, c, 0:half, :].astype(jnp.float32) * as_column(factor)
        out_ref[0, c] = (acc / as_column(total)).astype(out_ref.dtype)


def combine(parts):
    holders, requests, chunks, rows_in, lanes = parts.shape
    half = rows_in - 16
    return pl.pallas_call(
        combine_kernel,
        grid=(requests,),
        in_specs=[pl.BlockSpec((holders, 1, chunks, rows_in, lanes), lambda k: (0, k, 0, 0, 0))],
        out_specs=pl.BlockSpec((1, chunks, half, lanes), lambda k: (k, 0, 0, 0)),
        out_shape=jax.ShapeDtypeStruct((requests, chunks, half, lanes), jnp.bfloat16),
        compiler_params=pltpu.CompilerParams(dimension_semantics=("arbitrary",)),
        name="combine_holders",
    )(parts)


def finish_attention(attended, requests, tree_length):
    group = QUERY_HEADS // KEY_VALUE_HEADS
    chunks = attended.shape[1]
    shaped = attended.reshape(requests, chunks, group, tree_length, 2, 64)
    result = shaped.transpose(0, 3, 1, 4, 2, 5)
    return result.reshape(requests * tree_length, chunks * 2 * group * 64)


def rotate_flat(values, token_positions, head_columns):
    half_width = head_columns // 2
    frequency = THETA ** (-jnp.arange(half_width, dtype=jnp.float32) / half_width)
    angles = token_positions.astype(jnp.float32)[:, None] * frequency
    cosine = jnp.cos(angles)
    sines = jnp.sin(angles)
    repeats = values.shape[-1] // head_columns
    cosine = jnp.tile(jnp.concatenate([cosine, cosine], axis=-1), (1, repeats))
    sines = jnp.tile(jnp.concatenate([-sines, sines], axis=-1), (1, repeats))
    columns = jnp.arange(values.shape[-1], dtype=jnp.int32)
    front = (columns % head_columns) < half_width
    partner = jnp.where(
        front[None, :], jnp.roll(values, -half_width, axis=-1), jnp.roll(values, half_width, axis=-1)
    )
    return values * cosine + partner * sines


def body(
    hidden,
    norm_gain,
    w_qkv,
    w_out,
    ffn_gain,
    w_gate,
    w_up,
    w_down,
    cache,
    page_table,
    cache_len,
    parents,
    accept_leaf,
    page_slot,
):
    block_rows, draft_part, model_width = hidden.shape
    channels = w_qkv.shape[1]
    query_columns = w_out.shape[0]
    key_value_columns = (channels - query_columns) // 2
    req_count = lax.axis_size("req")
    rep_count = lax.axis_size("rep")
    rep_index = lax.axis_index("rep")
    requests = cache_len.shape[0]
    owner_page_count = requests // rep_count
    tree_length = parents.shape[1]
    own_start = rep_index * owner_page_count
    page_length = cache.shape[2]
    slots_count = page_table.shape[2]

    local_rows = hidden.reshape(owner_page_count, req_count, model_width)
    own_hidden = lax.all_to_all(local_rows, "req", split_axis=1, concat_axis=1, tiled=True)
    all_hidden = lax.all_gather(own_hidden, "rep", axis=0, tiled=True)

    normed = rms_scaled(all_hidden.astype(jnp.float32), norm_gain)
    projected = jnp.dot(
        normed.reshape(-1, model_width), w_qkv, preferred_element_type=jnp.float32
    ).astype(jnp.bfloat16).reshape(requests, tree_length, channels)

    reached = ancestors(parents)
    depths = jnp.sum(reached, axis=-1).astype(jnp.int32) - 1
    token_positions = cache_len[:, None] + depths
    flat_positions = token_positions.reshape(-1)
    head_columns = query_columns // QUERY_HEADS
    flat = projected.reshape(requests * tree_length, channels)
    queries = rotate_flat(
        flat[:, :query_columns].astype(jnp.float32), flat_positions, head_columns
    ).astype(jnp.bfloat16).reshape(requests, tree_length, query_columns)
    keys_all = rotate_flat(
        flat[:, query_columns : query_columns + key_value_columns].astype(jnp.float32),
        flat_positions,
        head_columns,
    ).astype(jnp.bfloat16).reshape(requests, tree_length, key_value_columns)
    values_all = projected[..., query_columns + key_value_columns :]

    page_list = page_table[:, 0, :]
    starts = (
        jnp.arange(slots_count, dtype=jnp.int32)[None, :] * rep_count + rep_index
    ) * page_length
    limits = cache_len[:, None] - starts
    mine = (jnp.arange(requests, dtype=jnp.int32) // owner_page_count) == rep_index
    draft_mask = jnp.where(mine[:, None, None], reached, 0.0)
    (parts,) = paged_partials(
        queries, cache, page_list, limits, keys_all, values_all, draft_mask
    )
    parts = parts.reshape((rep_count, owner_page_count) + parts.shape[1:])
    gathered = exchange(parts, rep_count, False, 1)
    attended = finish_attention(combine(gathered), owner_page_count, tree_length)

    mixed = jnp.dot(attended, w_out, preferred_element_type=jnp.float32)
    residual = (mixed + own_hidden.reshape(-1, model_width).astype(jnp.float32)).astype(
        jnp.bfloat16
    )
    residual_wide = residual.astype(jnp.float32)
    ffn_in = rms_scaled(residual_wide, ffn_gain).reshape(owner_page_count, tree_length, model_width)
    rows_in = exchange(ffn_in[None], rep_count, True, 2).reshape(-1, model_width)
    gate = jnp.dot(rows_in, w_gate, preferred_element_type=jnp.float32)
    up = jnp.dot(rows_in, w_up, preferred_element_type=jnp.float32)
    activated = (jax.nn.silu(gate) * up).astype(jnp.bfloat16)
    down = jnp.dot(activated, w_down, preferred_element_type=jnp.float32).reshape(
        rep_count, owner_page_count, tree_length, model_width
    )
    ffn_terms = exchange(down.astype(jnp.bfloat16), rep_count, False, 3)
    out_own = (
        jnp.sum(ffn_terms.astype(jnp.float32), axis=0)
        + residual_wide.reshape(owner_page_count, tree_length, model_width)
    ).astype(jnp.bfloat16)
    out = lax.all_to_all(out_own, "req", split_axis=1, concat_axis=1, tiled=True)
    out = out.reshape(block_rows, draft_part, model_width)

    all_rows = path_rows(keys_all, values_all, reached, depths, accept_leaf)
    new_pages = place_rows(all_rows, page_slot, own_start, owner_page_count)
    return (out, new_pages)


def solution(mesh):
    placed = (
        P("rep", "req", None),
        P(),
        P(),
        P(),
        P(),
        P(None, "rep"),
        P(None, "rep"),
        P("rep", None),
        P(("req", "rep"), None, None, None),
        P("req", "rep", None),
        P("req"),
        P("req", None),
        P("req"),
        P("req"),
    )
    return jax.shard_map(
        body,
        mesh=mesh,
        in_specs=placed,
        out_specs=(P("rep", "req", None), P(("req", "rep"), None, None, None)),
        check_vma=False,
    )
```

```python
import functools

import jax
import jax.numpy as jnp
from jax import lax
from jax.experimental import pallas as pl
from jax.experimental.pallas import tpu as pltpu
from jax.sharding import PartitionSpec as P

QUERY_HEADS = 18
KEY_VALUE_HEADS = 6
ACC = 8


SCALE = 0.125
EPSILON = 1e-05
THETA = 10000.0


def apply_rotation(values, token_positions, head_count):
    head_columns = values.shape[-1] // head_count
    half_width = head_columns // 2
    shaped = values.reshape(values.shape[:-1] + (head_count, head_columns))
    frequency = THETA ** (-jnp.arange(half_width, dtype=jnp.float32) / half_width)
    angles = token_positions.astype(jnp.float32)[..., None] * frequency
    cosine = jnp.cos(angles)[..., None, :]
    sines = jnp.sin(angles)[..., None, :]
    front_half = shaped[..., :half_width]
    back_half = shaped[..., half_width:]
    turned = jnp.concatenate(
        [front_half * cosine - back_half * sines, back_half * cosine + front_half * sines], axis=-1
    )
    return turned.reshape(values.shape)


def ancestors(parents):
    tree_length = parents.shape[-1]
    identity = jnp.eye(tree_length, dtype=jnp.float32)
    linked = jax.nn.one_hot(parents, tree_length, dtype=jnp.float32)
    reached = jnp.minimum(identity + linked, 1.0)
    for doubling in range(tree_length.bit_length()):
        reached = jnp.minimum(
            jnp.einsum("rts,rsu->rtu", reached, reached, precision=lax.Precision.HIGHEST), 1.0
        )
    return reached


def rms_scaled(values_in, gain):
    scaling = lax.rsqrt(jnp.mean(values_in * values_in, axis=-1, keepdims=True) + EPSILON)
    return (values_in * scaling * gain).astype(jnp.bfloat16)


def path_rows(key_matrix, value_matrix, reached, depths, leaf_ids):
    tree_length = reached.shape[-1]
    leaf_hot = jax.nn.one_hot(leaf_ids, tree_length, dtype=jnp.float32)
    on_path = jnp.einsum("rt,rts->rs", leaf_hot, reached, precision=lax.Precision.HIGHEST)
    level_hot = (depths[:, None, :] == jnp.arange(ACC, dtype=jnp.int32)[None, :, None]).astype(
        jnp.float32
    )
    selector = (on_path[:, None, :] * level_hot).astype(jnp.bfloat16)
    stacked = jnp.stack([key_matrix, value_matrix], axis=1)
    return jnp.einsum(
        "ras,rbsc->rbac", selector, stacked, preferred_element_type=jnp.float32
    ).astype(jnp.bfloat16)


def place_rows(rows, page_slot, own_start, owner_page_count):
    slot_ids = own_start + jnp.arange(owner_page_count, dtype=jnp.int32)
    chooser = (page_slot[None, :] == slot_ids[:, None]).astype(jnp.bfloat16)
    return jnp.einsum("pr,rbac->pbac", chooser, rows, preferred_element_type=jnp.float32).astype(
        jnp.bfloat16
    )


def paged_kernel(slots, chunks, page_ref, limit_ref, *refs):
    q_ref = refs[0]
    page_refs = refs[1 : 1 + slots]
    dk_ref, dv_ref, dmask_ref = refs[1 + slots : 4 + slots]
    (part_ref,) = refs[4 + slots :]
    request = pl.program_id(0)
    tree_length = q_ref.shape[1]
    page_length = page_refs[0].shape[2]
    rows = 6 * tree_length
    half = rows // 2
    low_t = lax.broadcasted_iota(jnp.int32, (tree_length, 128), 1) < 64
    low_h = lax.broadcasted_iota(jnp.int32, (half, 128), 1) < 64
    key_lanes = lax.broadcasted_iota(jnp.int32, (rows, slots * page_length), 1)
    key_slots = key_lanes // page_length
    limit_lanes = jnp.zeros_like(key_lanes)
    for s in range(slots):
        limit_lanes = jnp.where(key_slots == s, limit_ref[request, s], limit_lanes)
    cache_open = (key_lanes % page_length) < limit_lanes
    stat_lanes = lax.broadcasted_iota(jnp.int32, (rows, 128), 1)
    draft_open = jnp.concatenate([dmask_ref[0]] * 6, axis=0) > 0.5
    nt = (((1,), (1,)), ((), ()))
    for c in range(chunks):
        lanes = pl.ds(c * 128, 128)
        tiles = [q_ref[0, :, pl.ds(c * 384 + 128 * j, 128)].astype(jnp.float32) for j in range(3)]
        turned0 = pltpu.roll(tiles[0], 64, 1)
        turned2 = pltpu.roll(tiles[2], 64, 1)
        blocks = [
            jnp.where(low_t, tiles[0], 0.0),
            jnp.where(low_t, turned0, 0.0),
            jnp.where(low_t, tiles[1], 0.0),
            jnp.where(low_t, 0.0, tiles[1]),
            jnp.where(low_t, 0.0, turned2),
            jnp.where(low_t, 0.0, tiles[2]),
        ]
        qc = jnp.concatenate(blocks, axis=0).astype(jnp.bfloat16)
        keys = jnp.concatenate([page_refs[s][0, 0, :, lanes] for s in range(slots)], axis=0)
        values = jnp.concatenate([page_refs[s][0, 1, :, lanes] for s in range(slots)], axis=0)
        sc = lax.dot_general(qc, keys, nt, preferred_element_type=jnp.float32) * SCALE
        sc = jnp.where(cache_open, sc, -jnp.inf)
        kd = dk_ref[0, :, lanes]
        sd = lax.dot_general(qc, kd, nt, preferred_element_type=jnp.float32) * SCALE
        sd = jnp.where(draft_open, sd, -jnp.inf)
        peak = jnp.maximum(jnp.max(sd, axis=-1, keepdims=True), jnp.max(sc, axis=-1, keepdims=True))
        peak_hi = peak.astype(jnp.bfloat16).astype(jnp.float32)
        peak_lo = (peak - peak_hi).astype(jnp.bfloat16).astype(jnp.float32)
        peak = peak_hi + peak_lo
        wd = jnp.exp(sd - peak)
        ws = jnp.exp(sc - peak)
        total = jnp.sum(wd, axis=-1, keepdims=True) + jnp.sum(ws, axis=-1, keepdims=True)
        acc = jnp.dot(
            wd.astype(jnp.bfloat16), dv_ref[0, :, lanes], preferred_element_type=jnp.float32
        ) + jnp.dot(ws.astype(jnp.bfloat16), values, preferred_element_type=jnp.float32)
        part_ref[0, c, 0:half, :] = jnp.where(low_h, acc[:half], acc[half:]).astype(part_ref.dtype)
        stats = jnp.where(
            stat_lanes == 0,
            total,
            jnp.where(stat_lanes == 1, peak_hi, jnp.where(stat_lanes == 2, peak_lo, 0.0)),
        )
        flipped = jnp.transpose(stats)
        pieces = [flipped[j : j + 1, 128 * p : 128 * (p + 1)] for j in range(3) for p in range(3)]
        pieces.append(jnp.zeros((7, 128), jnp.float32))
        part_ref[0, c, half : half + 16, :] = jnp.concatenate(pieces, axis=0).astype(part_ref.dtype)


def paged_partials(queries, cache, page_list, limits, draft_keys, draft_values, draft_mask):
    requests, tree_length, query_columns = queries.shape
    chunks = KEY_VALUE_HEADS // 2
    rows = 6 * tree_length
    slots = page_list.shape[1]
    page_length = cache.shape[2]
    width = cache.shape[3]

    def page_map(s):
        return lambda k, pages, limit: (pages[k, s], 0, 0, 0)

    in_specs = [pl.BlockSpec((1, tree_length, query_columns), lambda k, pages, limit: (k, 0, 0))]
    in_specs += [pl.BlockSpec((1, 2, page_length, width), page_map(s)) for s in range(slots)]
    in_specs += [
        pl.BlockSpec((1, tree_length, width), lambda k, pages, limit: (k, 0, 0)),
        pl.BlockSpec((1, tree_length, width), lambda k, pages, limit: (k, 0, 0)),
        pl.BlockSpec((1, tree_length, tree_length), lambda k, pages, limit: (k, 0, 0)),
    ]
    out_specs = [
        pl.BlockSpec((1, chunks, rows // 2 + 16, 128), lambda k, pages, limit: (k, 0, 0, 0)),
    ]
    out_shape = [
        jax.ShapeDtypeStruct((requests, chunks, rows // 2 + 16, 128), jnp.bfloat16),
    ]
    keys_seen = slots * page_length + tree_length
    cost = pl.CostEstimate(
        flops=requests * chunks * rows * 128 * keys_seen * 4,
        bytes_accessed=requests * (slots * 2 * page_length * width * 2 + chunks * rows * 128 * 3),
        transcendentals=requests * chunks * rows * keys_seen,
    )
    grid_spec = pltpu.PrefetchScalarGridSpec(
        num_scalar_prefetch=2,
        grid=(requests,),
        in_specs=in_specs,
        out_specs=out_specs,
    )
    return pl.pallas_call(
        functools.partial(paged_kernel, slots, chunks),
        grid_spec=grid_spec,
        out_shape=out_shape,
        cost_estimate=cost,
        compiler_params=pltpu.CompilerParams(dimension_semantics=("arbitrary",)),
        name="paged_partials",
    )(page_list, limits, queries, *([cache] * slots), draft_keys, draft_values, draft_mask)


def exchange_kernel(count, same, x_ref, out_ref, local_sem, send_sems, recv_sems):
    me = lax.axis_index("rep")
    row = lax.axis_index("req")
    mesh_ids = pl.DeviceIdType.MESH
    barrier = pltpu.get_barrier_semaphore()
    for step in range(1, count):
        peer = lax.rem(me + step, count)
        pl.semaphore_signal(barrier, inc=1, device_id=(row, peer), device_id_type=mesh_ids)
    pl.semaphore_wait(barrier, count - 1)
    own = x_ref.at[0] if same else x_ref.at[me]
    local = pltpu.make_async_copy(own, out_ref.at[me], local_sem)
    local.start()
    sends = []
    for step in range(1, count):
        peer = lax.rem(me + step, count)
        source = x_ref.at[0] if same else x_ref.at[peer]
        copy = pltpu.make_async_remote_copy(
            src_ref=source,
            dst_ref=out_ref.at[me],
            send_sem=send_sems.at[step],
            recv_sem=recv_sems.at[step],
            device_id=(row, peer),
            device_id_type=mesh_ids,
        )
        copy.start()
        sends.append(copy)
    local.wait()
    for copy in sends:
        copy.wait_send()
    for step in range(1, count):
        origin = lax.rem(me + count - step, count)
        incoming = pltpu.make_async_remote_copy(
            src_ref=x_ref.at[0],
            dst_ref=out_ref.at[origin],
            send_sem=send_sems.at[step],
            recv_sem=recv_sems.at[step],
            device_id=(row, origin),
            device_id_type=mesh_ids,
        )
        incoming.wait_recv()


def exchange(blocks, count, same, collective_id):
    out_shape = jax.ShapeDtypeStruct((count,) + blocks.shape[1:], blocks.dtype)
    moved = blocks[0].size * blocks.dtype.itemsize * (count - 1)
    return pl.pallas_call(
        functools.partial(exchange_kernel, count, same),
        in_specs=[pl.BlockSpec(memory_space=pl.ANY)],
        out_specs=pl.BlockSpec(memory_space=pl.ANY),
        out_shape=out_shape,
        scratch_shapes=[
            pltpu.SemaphoreType.DMA(()),
            pltpu.SemaphoreType.DMA((count,)),
            pltpu.SemaphoreType.DMA((count,)),
        ],
        compiler_params=pltpu.CompilerParams(collective_id=collective_id, has_side_effects=True),
        cost_estimate=pl.CostEstimate(flops=0, bytes_accessed=2 * moved, transcendentals=0),
        name=f"exchange_{collective_id}",
    )(blocks)


def combine_kernel(part_ref, out_ref):
    holders, chunks = part_ref.shape[0], part_ref.shape[2]
    half = out_ref.shape[2]
    rows = 2 * half
    pieces = rows // 128
    low_h = lax.broadcasted_iota(jnp.int32, (half, 128), 1) < 64

    def as_column(row):
        column = jnp.transpose(jnp.broadcast_to(row, (128, rows)))
        return jnp.where(low_h, column[:half], column[half:])

    for c in range(chunks):
        tails = [
            part_ref[h, 0, c, half : half + 16, :].astype(jnp.float32) for h in range(holders)
        ]
        totals = [jnp.concatenate([t[p : p + 1] for p in range(pieces)], axis=1) for t in tails]
        peaks = [
            jnp.concatenate([t[pieces + p : pieces + p + 1] for p in range(pieces)], axis=1)
            + jnp.concatenate([t[2 * pieces + p : 2 * pieces + p + 1] for p in range(pieces)], axis=1)
            for t in tails
        ]
        top = peaks[0]
        for peak in peaks[1:]:
            top = jnp.maximum(top, peak)
        total = jnp.zeros_like(top)
        acc = jnp.zeros((half, 128), jnp.float32)
        for h in range(holders):
            factor = jnp.exp(peaks[h] - top)
            total = total + totals[h] * factor
            acc = acc + part_ref[h, 0, c, 0:half, :].astype(jnp.float32) * as_column(factor)
        out_ref[0, c] = (acc / as_column(total)).astype(out_ref.dtype)


def combine(parts):
    holders, requests, chunks, rows_in, lanes = parts.shape
    half = rows_in - 16
    return pl.pallas_call(
        combine_kernel,
        grid=(requests,),
        in_specs=[pl.BlockSpec((holders, 1, chunks, rows_in, lanes), lambda k: (0, k, 0, 0, 0))],
        out_specs=pl.BlockSpec((1, chunks, half, lanes), lambda k: (k, 0, 0, 0)),
        out_shape=jax.ShapeDtypeStruct((requests, chunks, half, lanes), jnp.bfloat16),
        compiler_params=pltpu.CompilerParams(dimension_semantics=("arbitrary",)),
        name="combine_holders",
    )(parts)


def finish_attention(attended, requests, tree_length):
    group = QUERY_HEADS // KEY_VALUE_HEADS
    chunks = attended.shape[1]
    shaped = attended.reshape(requests, chunks, group, tree_length, 2, 64)
    result = shaped.transpose(0, 3, 1, 4, 2, 5)
    return result.reshape(requests * tree_length, chunks * 2 * group * 64)


def rotate_flat(values, token_positions, head_columns):
    half_width = head_columns // 2
    frequency = THETA ** (-jnp.arange(half_width, dtype=jnp.float32) / half_width)
    angles = token_positions.astype(jnp.float32)[:, None] * frequency
    cosine = jnp.cos(angles)
    sines = jnp.sin(angles)
    repeats = values.shape[-1] // head_columns
    cosine = jnp.tile(jnp.concatenate([cosine, cosine], axis=-1), (1, repeats))
    sines = jnp.tile(jnp.concatenate([-sines, sines], axis=-1), (1, repeats))
    columns = jnp.arange(values.shape[-1], dtype=jnp.int32)
    front = (columns % head_columns) < half_width
    partner = jnp.where(
        front[None, :], jnp.roll(values, -half_width, axis=-1), jnp.roll(values, half_width, axis=-1)
    )
    return values * cosine + partner * sines


def body(
    hidden,
    norm_gain,
    w_qkv,
    w_out,
    ffn_gain,
    w_gate,
    w_up,
    w_down,
    cache,
    page_table,
    cache_len,
    parents,
    accept_leaf,
    page_slot,
):
    block_rows, draft_part, model_width = hidden.shape
    channels = w_qkv.shape[1]
    query_columns = w_out.shape[0]
    key_value_columns = (channels - query_columns) // 2
    req_count = lax.axis_size("req")
    rep_count = lax.axis_size("rep")
    rep_index = lax.axis_index("rep")
    requests = cache_len.shape[0]
    owner_page_count = requests // rep_count
    tree_length = parents.shape[1]
    own_start = rep_index * owner_page_count
    page_length = cache.shape[2]
    slots_count = page_table.shape[2]

    local_rows = hidden.reshape(owner_page_count, req_count, model_width)
    own_hidden = lax.all_to_all(local_rows, "req", split_axis=1, concat_axis=1, tiled=True)
    all_hidden = lax.all_gather(own_hidden, "rep", axis=0, tiled=True)

    normed = rms_scaled(all_hidden.astype(jnp.float32), norm_gain)
    projected = jnp.dot(
        normed.reshape(-1, model_width), w_qkv, preferred_element_type=jnp.float32
    ).astype(jnp.bfloat16).reshape(requests, tree_length, channels)

    reached = ancestors(parents)
    depths = jnp.sum(reached, axis=-1).astype(jnp.int32) - 1
    token_positions = cache_len[:, None] + depths
    flat_positions = token_positions.reshape(-1)
    head_columns = query_columns // QUERY_HEADS
    flat = projected.reshape(requests * tree_length, channels)
    queries = rotate_flat(
        flat[:, :query_columns].astype(jnp.float32), flat_positions, head_columns
    ).astype(jnp.bfloat16).reshape(requests, tree_length, query_columns)
    keys_all = rotate_flat(
        flat[:, query_columns : query_columns + key_value_columns].astype(jnp.float32),
        flat_positions,
        head_columns,
    ).astype(jnp.bfloat16).reshape(requests, tree_length, key_value_columns)
    values_all = projected[..., query_columns + key_value_columns :]

    page_list = page_table[:, 0, :]
    starts = (
        jnp.arange(slots_count, dtype=jnp.int32)[None, :] * rep_count + rep_index
    ) * page_length
    limits = cache_len[:, None] - starts
    mine = (jnp.arange(requests, dtype=jnp.int32) // owner_page_count) == rep_index
    draft_mask = jnp.where(mine[:, None, None], reached, 0.0)
    (parts,) = paged_partials(
        queries, cache, page_list, limits, keys_all, values_all, draft_mask
    )
    parts = parts.reshape((rep_count, owner_page_count) + parts.shape[1:])
    gathered = exchange(parts, rep_count, False, 1)
    attended = finish_attention(combine(gathered), owner_page_count, tree_length)

    mixed = jnp.dot(attended, w_out, preferred_element_type=jnp.float32)
    residual = (mixed + own_hidden.reshape(-1, model_width).astype(jnp.float32)).astype(
        jnp.bfloat16
    )
    residual_wide = residual.astype(jnp.float32)
    ffn_in = rms_scaled(residual_wide, ffn_gain).reshape(owner_page_count, tree_length, model_width)
    rows_in = exchange(ffn_in[None], rep_count, True, 2).reshape(-1, model_width)
    gate = jnp.dot(rows_in, w_gate, preferred_element_type=jnp.float32)
    up = jnp.dot(rows_in, w_up, preferred_element_type=jnp.float32)
    activated = (jax.nn.silu(gate) * up).astype(jnp.bfloat16)
    down = jnp.dot(activated, w_down, preferred_element_type=jnp.float32).reshape(
        rep_count, owner_page_count, tree_length, model_width
    )
    ffn_terms = exchange(down.astype(jnp.bfloat16), rep_count, False, 3)
    out_own = (
        jnp.sum(ffn_terms.astype(jnp.float32), axis=0)
        + residual_wide.reshape(owner_page_count, tree_length, model_width)
    ).astype(jnp.bfloat16)
    out = lax.all_to_all(out_own, "req", split_axis=1, concat_axis=1, tiled=True)
    out = out.reshape(block_rows, draft_part, model_width)

    all_rows = path_rows(keys_all, values_all, reached, depths, accept_leaf)
    new_pages = place_rows(all_rows, page_slot, own_start, owner_page_count)
    return (out, new_pages)


def solution(mesh):
    placed = (
        P("rep", "req", None),
        P(),
        P(),
        P(),
        P(),
        P(None, "rep"),
        P(None, "rep"),
        P("rep", None),
        P(("req", "rep"), None, None, None),
        P("req", "rep", None),
        P("req"),
        P("req", None),
        P("req"),
        P("req"),
    )
    return jax.shard_map(
        body,
        mesh=mesh,
        in_specs=placed,
        out_specs=(P("rep", "req", None), P(("req", "rep"), None, None, None)),
        check_vma=False,
    )
```

```python
import functools

import jax
import jax.numpy as jnp
from jax import lax
from jax.experimental import pallas as pl
from jax.experimental.pallas import tpu as pltpu
from jax.sharding import PartitionSpec as P

QUERY_HEADS = 18
KEY_VALUE_HEADS = 6
ACC = 8


SCALE = 0.125
EPSILON = 1e-05
THETA = 10000.0


def apply_rotation(values, token_positions, head_count):
    head_columns = values.shape[-1] // head_count
    half_width = head_columns // 2
    shaped = values.reshape(values.shape[:-1] + (head_count, head_columns))
    frequency = THETA ** (-jnp.arange(half_width, dtype=jnp.float32) / half_width)
    angles = token_positions.astype(jnp.float32)[..., None] * frequency
    cosine = jnp.cos(angles)[..., None, :]
    sines = jnp.sin(angles)[..., None, :]
    front_half = shaped[..., :half_width]
    back_half = shaped[..., half_width:]
    turned = jnp.concatenate(
        [front_half * cosine - back_half * sines, back_half * cosine + front_half * sines], axis=-1
    )
    return turned.reshape(values.shape)


def ancestors(parents):
    tree_length = parents.shape[-1]
    identity = jnp.eye(tree_length, dtype=jnp.float32)
    linked = jax.nn.one_hot(parents, tree_length, dtype=jnp.float32)
    reached = jnp.minimum(identity + linked, 1.0)
    for doubling in range(tree_length.bit_length()):
        reached = jnp.minimum(
            jnp.einsum("rts,rsu->rtu", reached, reached, precision=lax.Precision.HIGHEST), 1.0
        )
    return reached


def rms_scaled(values_in, gain):
    scaling = lax.rsqrt(jnp.mean(values_in * values_in, axis=-1, keepdims=True) + EPSILON)
    return (values_in * scaling * gain).astype(jnp.bfloat16)


def path_rows(key_matrix, value_matrix, reached, depths, leaf_ids):
    tree_length = reached.shape[-1]
    leaf_hot = jax.nn.one_hot(leaf_ids, tree_length, dtype=jnp.float32)
    on_path = jnp.einsum("rt,rts->rs", leaf_hot, reached, precision=lax.Precision.HIGHEST)
    level_hot = (depths[:, None, :] == jnp.arange(ACC, dtype=jnp.int32)[None, :, None]).astype(
        jnp.float32
    )
    selector = (on_path[:, None, :] * level_hot).astype(jnp.bfloat16)
    stacked = jnp.stack([key_matrix, value_matrix], axis=1)
    return jnp.einsum(
        "ras,rbsc->rbac", selector, stacked, preferred_element_type=jnp.float32
    ).astype(jnp.bfloat16)


def place_rows(rows, page_slot, own_start, owner_page_count):
    slot_ids = own_start + jnp.arange(owner_page_count, dtype=jnp.int32)
    chooser = (page_slot[None, :] == slot_ids[:, None]).astype(jnp.bfloat16)
    return jnp.einsum("pr,rbac->pbac", chooser, rows, preferred_element_type=jnp.float32).astype(
        jnp.bfloat16
    )


def paged_kernel(slots, chunks, page_ref, limit_ref, *refs):
    q_ref = refs[0]
    page_refs = refs[1 : 1 + slots]
    dk_ref, dv_ref, dmask_ref = refs[1 + slots : 4 + slots]
    (part_ref,) = refs[4 + slots :]
    request = pl.program_id(0)
    tree_length = q_ref.shape[1]
    page_length = page_refs[0].shape[2]
    rows = 6 * tree_length
    half = rows // 2
    low_t = lax.broadcasted_iota(jnp.int32, (tree_length, 128), 1) < 64
    low_h = lax.broadcasted_iota(jnp.int32, (half, 128), 1) < 64
    key_lanes = lax.broadcasted_iota(jnp.int32, (rows, slots * page_length), 1)
    key_slots = key_lanes // page_length
    limit_lanes = jnp.zeros_like(key_lanes)
    for s in range(slots):
        limit_lanes = jnp.where(key_slots == s, limit_ref[request, s], limit_lanes)
    cache_open = (key_lanes % page_length) < limit_lanes
    stat_lanes = lax.broadcasted_iota(jnp.int32, (rows, 128), 1)
    draft_open = jnp.concatenate([dmask_ref[0]] * 6, axis=0) > 0.5
    nt = (((1,), (1,)), ((), ()))
    for c in range(chunks):
        lanes = pl.ds(c * 128, 128)
        tiles = [q_ref[0, :, pl.ds(c * 384 + 128 * j, 128)].astype(jnp.float32) for j in range(3)]
        turned0 = pltpu.roll(tiles[0], 64, 1)
        turned2 = pltpu.roll(tiles[2], 64, 1)
        blocks = [
            jnp.where(low_t, tiles[0], 0.0),
            jnp.where(low_t, turned0, 0.0),
            jnp.where(low_t, tiles[1], 0.0),
            jnp.where(low_t, 0.0, tiles[1]),
            jnp.where(low_t, 0.0, turned2),
            jnp.where(low_t, 0.0, tiles[2]),
        ]
        qc = (jnp.concatenate(blocks, axis=0) * SCALE).astype(jnp.bfloat16)
        keys = jnp.concatenate([page_refs[s][0, 0, :, lanes] for s in range(slots)], axis=0)
        values = jnp.concatenate([page_refs[s][0, 1, :, lanes] for s in range(slots)], axis=0)
        sc = lax.dot_general(qc, keys, nt, preferred_element_type=jnp.float32)
        sc = jnp.where(cache_open, sc, -jnp.inf)
        kd = dk_ref[0, :, lanes]
        sd = lax.dot_general(qc, kd, nt, preferred_element_type=jnp.float32)
        sd = jnp.where(draft_open, sd, -jnp.inf)
        peak = jnp.maximum(jnp.max(sd, axis=-1, keepdims=True), jnp.max(sc, axis=-1, keepdims=True))
        peak_hi = peak.astype(jnp.bfloat16).astype(jnp.float32)
        peak_lo = (peak - peak_hi).astype(jnp.bfloat16).astype(jnp.float32)
        peak = peak_hi + peak_lo
        wd = jnp.exp(sd - peak)
        ws = jnp.exp(sc - peak)
        total = jnp.sum(wd, axis=-1, keepdims=True) + jnp.sum(ws, axis=-1, keepdims=True)
        acc = jnp.dot(
            wd.astype(jnp.bfloat16), dv_ref[0, :, lanes], preferred_element_type=jnp.float32
        ) + jnp.dot(ws.astype(jnp.bfloat16), values, preferred_element_type=jnp.float32)
        part_ref[0, c, 0:half, :] = jnp.where(low_h, acc[:half], acc[half:]).astype(part_ref.dtype)
        stats = jnp.where(
            stat_lanes == 0,
            total,
            jnp.where(stat_lanes == 1, peak_hi, jnp.where(stat_lanes == 2, peak_lo, 0.0)),
        )
        flipped = jnp.transpose(stats)
        pieces = [flipped[j : j + 1, 128 * p : 128 * (p + 1)] for j in range(3) for p in range(3)]
        pieces.append(jnp.zeros((7, 128), jnp.float32))
        part_ref[0, c, half : half + 16, :] = jnp.concatenate(pieces, axis=0).astype(part_ref.dtype)


def paged_partials(queries, cache, page_list, limits, draft_keys, draft_values, draft_mask):
    requests, tree_length, query_columns = queries.shape
    chunks = KEY_VALUE_HEADS // 2
    rows = 6 * tree_length
    slots = page_list.shape[1]
    page_length = cache.shape[2]
    width = cache.shape[3]

    def page_map(s):
        return lambda k, pages, limit: (pages[k, s], 0, 0, 0)

    in_specs = [pl.BlockSpec((1, tree_length, query_columns), lambda k, pages, limit: (k, 0, 0))]
    in_specs += [pl.BlockSpec((1, 2, page_length, width), page_map(s)) for s in range(slots)]
    in_specs += [
        pl.BlockSpec((1, tree_length, width), lambda k, pages, limit: (k, 0, 0)),
        pl.BlockSpec((1, tree_length, width), lambda k, pages, limit: (k, 0, 0)),
        pl.BlockSpec((1, tree_length, tree_length), lambda k, pages, limit: (k, 0, 0)),
    ]
    out_specs = [
        pl.BlockSpec((1, chunks, rows // 2 + 16, 128), lambda k, pages, limit: (k, 0, 0, 0)),
    ]
    out_shape = [
        jax.ShapeDtypeStruct((requests, chunks, rows // 2 + 16, 128), jnp.bfloat16),
    ]
    keys_seen = slots * page_length + tree_length
    cost = pl.CostEstimate(
        flops=requests * chunks * rows * 128 * keys_seen * 4,
        bytes_accessed=requests * (slots * 2 * page_length * width * 2 + chunks * rows * 128 * 3),
        transcendentals=requests * chunks * rows * keys_seen,
    )
    grid_spec = pltpu.PrefetchScalarGridSpec(
        num_scalar_prefetch=2,
        grid=(requests,),
        in_specs=in_specs,
        out_specs=out_specs,
    )
    return pl.pallas_call(
        functools.partial(paged_kernel, slots, chunks),
        grid_spec=grid_spec,
        out_shape=out_shape,
        cost_estimate=cost,
        compiler_params=pltpu.CompilerParams(dimension_semantics=("arbitrary",)),
        name="paged_partials",
    )(page_list, limits, queries, *([cache] * slots), draft_keys, draft_values, draft_mask)


def exchange_kernel(count, same, x_ref, out_ref, local_sem, send_sems, recv_sems):
    me = lax.axis_index("rep")
    row = lax.axis_index("req")
    mesh_ids = pl.DeviceIdType.MESH
    barrier = pltpu.get_barrier_semaphore()
    for step in range(1, count):
        peer = lax.rem(me + step, count)
        pl.semaphore_signal(barrier, inc=1, device_id=(row, peer), device_id_type=mesh_ids)
    pl.semaphore_wait(barrier, count - 1)
    own = x_ref.at[0] if same else x_ref.at[me]
    local = pltpu.make_async_copy(own, out_ref.at[me], local_sem)
    local.start()
    sends = []
    for step in range(1, count):
        peer = lax.rem(me + step, count)
        source = x_ref.at[0] if same else x_ref.at[peer]
        copy = pltpu.make_async_remote_copy(
            src_ref=source,
            dst_ref=out_ref.at[me],
            send_sem=send_sems.at[step],
            recv_sem=recv_sems.at[step],
            device_id=(row, peer),
            device_id_type=mesh_ids,
        )
        copy.start()
        sends.append(copy)
    local.wait()
    for copy in sends:
        copy.wait_send()
    for step in range(1, count):
        origin = lax.rem(me + count - step, count)
        incoming = pltpu.make_async_remote_copy(
            src_ref=x_ref.at[0],
            dst_ref=out_ref.at[origin],
            send_sem=send_sems.at[step],
            recv_sem=recv_sems.at[step],
            device_id=(row, origin),
            device_id_type=mesh_ids,
        )
        incoming.wait_recv()


def exchange(blocks, count, same, collective_id):
    out_shape = jax.ShapeDtypeStruct((count,) + blocks.shape[1:], blocks.dtype)
    moved = blocks[0].size * blocks.dtype.itemsize * (count - 1)
    return pl.pallas_call(
        functools.partial(exchange_kernel, count, same),
        in_specs=[pl.BlockSpec(memory_space=pl.ANY)],
        out_specs=pl.BlockSpec(memory_space=pl.ANY),
        out_shape=out_shape,
        scratch_shapes=[
            pltpu.SemaphoreType.DMA(()),
            pltpu.SemaphoreType.DMA((count,)),
            pltpu.SemaphoreType.DMA((count,)),
        ],
        compiler_params=pltpu.CompilerParams(collective_id=collective_id, has_side_effects=True),
        cost_estimate=pl.CostEstimate(flops=0, bytes_accessed=2 * moved, transcendentals=0),
        name=f"exchange_{collective_id}",
    )(blocks)


def combine_kernel(part_ref, out_ref):
    holders, chunks = part_ref.shape[0], part_ref.shape[2]
    half = out_ref.shape[2]
    rows = 2 * half
    pieces = rows // 128
    low_h = lax.broadcasted_iota(jnp.int32, (half, 128), 1) < 64

    def as_column(row):
        column = jnp.transpose(jnp.broadcast_to(row, (128, rows)))
        return jnp.where(low_h, column[:half], column[half:])

    for c in range(chunks):
        tails = [
            part_ref[h, 0, c, half : half + 16, :].astype(jnp.float32) for h in range(holders)
        ]
        totals = [jnp.concatenate([t[p : p + 1] for p in range(pieces)], axis=1) for t in tails]
        peaks = [
            jnp.concatenate([t[pieces + p : pieces + p + 1] for p in range(pieces)], axis=1)
            + jnp.concatenate([t[2 * pieces + p : 2 * pieces + p + 1] for p in range(pieces)], axis=1)
            for t in tails
        ]
        top = peaks[0]
        for peak in peaks[1:]:
            top = jnp.maximum(top, peak)
        total = jnp.zeros_like(top)
        acc = jnp.zeros((half, 128), jnp.float32)
        for h in range(holders):
            factor = jnp.exp(peaks[h] - top)
            total = total + totals[h] * factor
            acc = acc + part_ref[h, 0, c, 0:half, :].astype(jnp.float32) * as_column(factor)
        out_ref[0, c] = (acc / as_column(total)).astype(out_ref.dtype)


def combine(parts):
    holders, requests, chunks, rows_in, lanes = parts.shape
    half = rows_in - 16
    return pl.pallas_call(
        combine_kernel,
        grid=(requests,),
        in_specs=[pl.BlockSpec((holders, 1, chunks, rows_in, lanes), lambda k: (0, k, 0, 0, 0))],
        out_specs=pl.BlockSpec((1, chunks, half, lanes), lambda k: (k, 0, 0, 0)),
        out_shape=jax.ShapeDtypeStruct((requests, chunks, half, lanes), jnp.bfloat16),
        compiler_params=pltpu.CompilerParams(dimension_semantics=("arbitrary",)),
        name="combine_holders",
    )(parts)


def finish_attention(attended, requests, tree_length):
    group = QUERY_HEADS // KEY_VALUE_HEADS
    chunks = attended.shape[1]
    shaped = attended.reshape(requests, chunks, group, tree_length, 2, 64)
    result = shaped.transpose(0, 3, 1, 4, 2, 5)
    return result.reshape(requests * tree_length, chunks * 2 * group * 64)


def rotate_flat(values, token_positions, head_columns):
    half_width = head_columns // 2
    frequency = THETA ** (-jnp.arange(half_width, dtype=jnp.float32) / half_width)
    angles = token_positions.astype(jnp.float32)[:, None] * frequency
    cosine = jnp.cos(angles)
    sines = jnp.sin(angles)
    repeats = values.shape[-1] // head_columns
    cosine = jnp.tile(jnp.concatenate([cosine, cosine], axis=-1), (1, repeats))
    sines = jnp.tile(jnp.concatenate([-sines, sines], axis=-1), (1, repeats))
    columns = jnp.arange(values.shape[-1], dtype=jnp.int32)
    front = (columns % head_columns) < half_width
    partner = jnp.where(
        front[None, :], jnp.roll(values, -half_width, axis=-1), jnp.roll(values, half_width, axis=-1)
    )
    return values * cosine + partner * sines


def body(
    hidden,
    norm_gain,
    w_qkv,
    w_out,
    ffn_gain,
    w_gate,
    w_up,
    w_down,
    cache,
    page_table,
    cache_len,
    parents,
    accept_leaf,
    page_slot,
):
    block_rows, draft_part, model_width = hidden.shape
    channels = w_qkv.shape[1]
    query_columns = w_out.shape[0]
    key_value_columns = (channels - query_columns) // 2
    req_count = lax.axis_size("req")
    rep_count = lax.axis_size("rep")
    rep_index = lax.axis_index("rep")
    requests = cache_len.shape[0]
    owner_page_count = requests // rep_count
    tree_length = parents.shape[1]
    own_start = rep_index * owner_page_count
    page_length = cache.shape[2]
    slots_count = page_table.shape[2]

    local_rows = hidden.reshape(owner_page_count, req_count, model_width)
    own_hidden = lax.all_to_all(local_rows, "req", split_axis=1, concat_axis=1, tiled=True)
    all_hidden = lax.all_gather(own_hidden, "rep", axis=0, tiled=True)

    normed = rms_scaled(all_hidden.astype(jnp.float32), norm_gain)
    projected = jnp.dot(
        normed.reshape(-1, model_width), w_qkv, preferred_element_type=jnp.float32
    ).astype(jnp.bfloat16).reshape(requests, tree_length, channels)

    reached = ancestors(parents)
    depths = jnp.sum(reached, axis=-1).astype(jnp.int32) - 1
    token_positions = cache_len[:, None] + depths
    flat_positions = token_positions.reshape(-1)
    head_columns = query_columns // QUERY_HEADS
    flat = projected.reshape(requests * tree_length, channels)
    queries = rotate_flat(
        flat[:, :query_columns].astype(jnp.float32), flat_positions, head_columns
    ).astype(jnp.bfloat16).reshape(requests, tree_length, query_columns)
    keys_all = rotate_flat(
        flat[:, query_columns : query_columns + key_value_columns].astype(jnp.float32),
        flat_positions,
        head_columns,
    ).astype(jnp.bfloat16).reshape(requests, tree_length, key_value_columns)
    values_all = projected[..., query_columns + key_value_columns :]

    page_list = page_table[:, 0, :]
    starts = (
        jnp.arange(slots_count, dtype=jnp.int32)[None, :] * rep_count + rep_index
    ) * page_length
    limits = cache_len[:, None] - starts
    mine = (jnp.arange(requests, dtype=jnp.int32) // owner_page_count) == rep_index
    draft_mask = jnp.where(mine[:, None, None], reached, 0.0)
    (parts,) = paged_partials(
        queries, cache, page_list, limits, keys_all, values_all, draft_mask
    )
    parts = parts.reshape((rep_count, owner_page_count) + parts.shape[1:])
    gathered = exchange(parts, rep_count, False, 1)
    attended = finish_attention(combine(gathered), owner_page_count, tree_length)

    mixed = jnp.dot(attended, w_out, preferred_element_type=jnp.float32)
    residual = (mixed + own_hidden.reshape(-1, model_width).astype(jnp.float32)).astype(
        jnp.bfloat16
    )
    residual_wide = residual.astype(jnp.float32)
    ffn_in = rms_scaled(residual_wide, ffn_gain).reshape(owner_page_count, tree_length, model_width)
    rows_in = exchange(ffn_in[None], rep_count, True, 2).reshape(-1, model_width)
    gate = jnp.dot(rows_in, w_gate, preferred_element_type=jnp.float32)
    up = jnp.dot(rows_in, w_up, preferred_element_type=jnp.float32)
    activated = (jax.nn.silu(gate) * up).astype(jnp.bfloat16)
    down = jnp.dot(activated, w_down, preferred_element_type=jnp.float32).reshape(
        rep_count, owner_page_count, tree_length, model_width
    )
    ffn_terms = exchange(down.astype(jnp.bfloat16), rep_count, False, 3)
    out_own = (
        jnp.sum(ffn_terms.astype(jnp.float32), axis=0)
        + residual_wide.reshape(owner_page_count, tree_length, model_width)
    ).astype(jnp.bfloat16)
    out = lax.all_to_all(out_own, "req", split_axis=1, concat_axis=1, tiled=True)
    out = out.reshape(block_rows, draft_part, model_width)

    all_rows = path_rows(keys_all, values_all, reached, depths, accept_leaf)
    new_pages = place_rows(all_rows, page_slot, own_start, owner_page_count)
    return (out, new_pages)


def solution(mesh):
    placed = (
        P("rep", "req", None),
        P(),
        P(),
        P(),
        P(),
        P(None, "rep"),
        P(None, "rep"),
        P("rep", None),
        P(("req", "rep"), None, None, None),
        P("req", "rep", None),
        P("req"),
        P("req", None),
        P("req"),
        P("req"),
    )
    return jax.shard_map(
        body,
        mesh=mesh,
        in_specs=placed,
        out_specs=(P("rep", "req", None), P(("req", "rep"), None, None, None)),
        check_vma=False,
    )
```

```python
import functools

import jax
import jax.numpy as jnp
from jax import lax
from jax.experimental import pallas as pl
from jax.experimental.pallas import tpu as pltpu
from jax.sharding import PartitionSpec as P

QUERY_HEADS = 18
KEY_VALUE_HEADS = 6
ACC = 8


SCALE = 0.125
EPSILON = 1e-05
THETA = 10000.0


def apply_rotation(values, token_positions, head_count):
    head_columns = values.shape[-1] // head_count
    half_width = head_columns // 2
    shaped = values.reshape(values.shape[:-1] + (head_count, head_columns))
    frequency = THETA ** (-jnp.arange(half_width, dtype=jnp.float32) / half_width)
    angles = token_positions.astype(jnp.float32)[..., None] * frequency
    cosine = jnp.cos(angles)[..., None, :]
    sines = jnp.sin(angles)[..., None, :]
    front_half = shaped[..., :half_width]
    back_half = shaped[..., half_width:]
    turned = jnp.concatenate(
        [front_half * cosine - back_half * sines, back_half * cosine + front_half * sines], axis=-1
    )
    return turned.reshape(values.shape)


def ancestors(parents):
    tree_length = parents.shape[-1]
    identity = jnp.eye(tree_length, dtype=jnp.float32)
    linked = jax.nn.one_hot(parents, tree_length, dtype=jnp.float32)
    reached = jnp.minimum(identity + linked, 1.0)
    for doubling in range(tree_length.bit_length()):
        reached = jnp.minimum(
            jnp.einsum("rts,rsu->rtu", reached, reached, precision=lax.Precision.HIGHEST), 1.0
        )
    return reached


def rms_scaled(values_in, gain):
    scaling = lax.rsqrt(jnp.mean(values_in * values_in, axis=-1, keepdims=True) + EPSILON)
    return (values_in * scaling * gain).astype(jnp.bfloat16)


def path_rows(key_matrix, value_matrix, reached, depths, leaf_ids):
    tree_length = reached.shape[-1]
    leaf_hot = jax.nn.one_hot(leaf_ids, tree_length, dtype=jnp.float32)
    on_path = jnp.einsum("rt,rts->rs", leaf_hot, reached, precision=lax.Precision.HIGHEST)
    level_hot = (depths[:, None, :] == jnp.arange(ACC, dtype=jnp.int32)[None, :, None]).astype(
        jnp.float32
    )
    selector = (on_path[:, None, :] * level_hot).astype(jnp.bfloat16)
    stacked = jnp.stack([key_matrix, value_matrix], axis=1)
    return jnp.einsum(
        "ras,rbsc->rbac", selector, stacked, preferred_element_type=jnp.float32
    ).astype(jnp.bfloat16)


def place_rows(rows, page_slot, own_start, owner_page_count):
    slot_ids = own_start + jnp.arange(owner_page_count, dtype=jnp.int32)
    chooser = (page_slot[None, :] == slot_ids[:, None]).astype(jnp.bfloat16)
    return jnp.einsum("pr,rbac->pbac", chooser, rows, preferred_element_type=jnp.float32).astype(
        jnp.bfloat16
    )


def paged_kernel(slots, chunks, page_ref, limit_ref, *refs):
    q_ref = refs[0]
    page_refs = refs[1 : 1 + slots]
    dk_ref, dv_ref, dmask_ref = refs[1 + slots : 4 + slots]
    (part_ref,) = refs[4 + slots :]
    request = pl.program_id(0)
    tree_length = q_ref.shape[1]
    page_length = page_refs[0].shape[2]
    rows = 6 * tree_length
    half = rows // 2
    low_t = lax.broadcasted_iota(jnp.int32, (tree_length, 128), 1) < 64
    low_h = lax.broadcasted_iota(jnp.int32, (half, 128), 1) < 64
    key_lanes = lax.broadcasted_iota(jnp.int32, (rows, slots * page_length), 1)
    key_slots = key_lanes // page_length
    limit_lanes = jnp.zeros_like(key_lanes)
    for s in range(slots):
        limit_lanes = jnp.where(key_slots == s, limit_ref[request, s], limit_lanes)
    cache_open = (key_lanes % page_length) < limit_lanes
    stat_lanes = lax.broadcasted_iota(jnp.int32, (rows, 128), 1)
    draft_open = jnp.concatenate([dmask_ref[0]] * 6, axis=0) > 0.5
    nt = (((1,), (1,)), ((), ()))
    for c in range(chunks):
        lanes = pl.ds(c * 128, 128)
        tiles = [q_ref[0, :, pl.ds(c * 384 + 128 * j, 128)].astype(jnp.float32) for j in range(3)]
        turned0 = pltpu.roll(tiles[0], 64, 1)
        turned2 = pltpu.roll(tiles[2], 64, 1)
        blocks = [
            jnp.where(low_t, tiles[0], 0.0),
            jnp.where(low_t, turned0, 0.0),
            jnp.where(low_t, tiles[1], 0.0),
            jnp.where(low_t, 0.0, tiles[1]),
            jnp.where(low_t, 0.0, turned2),
            jnp.where(low_t, 0.0, tiles[2]),
        ]
        qc = (jnp.concatenate(blocks, axis=0) * SCALE).astype(jnp.bfloat16)
        keys = jnp.concatenate([page_refs[s][0, 0, :, lanes] for s in range(slots)], axis=0)
        values = jnp.concatenate([page_refs[s][0, 1, :, lanes] for s in range(slots)], axis=0)
        sc = lax.dot_general(qc, keys, nt, preferred_element_type=jnp.float32)
        sc = jnp.where(cache_open, sc, -jnp.inf)
        kd = dk_ref[0, :, lanes]
        sd = lax.dot_general(qc, kd, nt, preferred_element_type=jnp.float32)
        sd = jnp.where(draft_open, sd, -jnp.inf)
        peak = jnp.maximum(jnp.max(sd, axis=-1, keepdims=True), jnp.max(sc, axis=-1, keepdims=True))
        peak_hi = peak.astype(jnp.bfloat16).astype(jnp.float32)
        peak_lo = (peak - peak_hi).astype(jnp.bfloat16).astype(jnp.float32)
        peak = peak_hi + peak_lo
        wd = jnp.exp(sd - peak)
        ws = jnp.exp(sc - peak)
        total = jnp.sum(wd, axis=-1, keepdims=True) + jnp.sum(ws, axis=-1, keepdims=True)
        acc = jnp.dot(
            wd.astype(jnp.bfloat16), dv_ref[0, :, lanes], preferred_element_type=jnp.float32
        ) + jnp.dot(ws.astype(jnp.bfloat16), values, preferred_element_type=jnp.float32)
        part_ref[0, c, 0:half, :] = jnp.where(low_h, acc[:half], acc[half:]).astype(part_ref.dtype)
        stats = jnp.where(
            stat_lanes == 0,
            total,
            jnp.where(stat_lanes == 1, peak_hi, jnp.where(stat_lanes == 2, peak_lo, 0.0)),
        )
        flipped = jnp.transpose(stats)
        pieces = [flipped[j : j + 1, 128 * p : 128 * (p + 1)] for j in range(3) for p in range(3)]
        pieces.append(jnp.zeros((7, 128), jnp.float32))
        part_ref[0, c, half : half + 16, :] = jnp.concatenate(pieces, axis=0).astype(part_ref.dtype)


def paged_partials(queries, cache, page_list, limits, draft_keys, draft_values, draft_mask):
    requests, tree_length, query_columns = queries.shape
    chunks = KEY_VALUE_HEADS // 2
    rows = 6 * tree_length
    slots = page_list.shape[1]
    page_length = cache.shape[2]
    width = cache.shape[3]

    def page_map(s):
        return lambda k, pages, limit: (pages[k, s], 0, 0, 0)

    in_specs = [pl.BlockSpec((1, tree_length, query_columns), lambda k, pages, limit: (k, 0, 0))]
    in_specs += [pl.BlockSpec((1, 2, page_length, width), page_map(s)) for s in range(slots)]
    in_specs += [
        pl.BlockSpec((1, tree_length, width), lambda k, pages, limit: (k, 0, 0)),
        pl.BlockSpec((1, tree_length, width), lambda k, pages, limit: (k, 0, 0)),
        pl.BlockSpec((1, tree_length, tree_length), lambda k, pages, limit: (k, 0, 0)),
    ]
    out_specs = [
        pl.BlockSpec((1, chunks, rows // 2 + 16, 128), lambda k, pages, limit: (k, 0, 0, 0)),
    ]
    out_shape = [
        jax.ShapeDtypeStruct((requests, chunks, rows // 2 + 16, 128), jnp.bfloat16),
    ]
    keys_seen = slots * page_length + tree_length
    cost = pl.CostEstimate(
        flops=requests * chunks * rows * 128 * keys_seen * 4,
        bytes_accessed=requests * (slots * 2 * page_length * width * 2 + chunks * rows * 128 * 3),
        transcendentals=requests * chunks * rows * keys_seen,
    )
    grid_spec = pltpu.PrefetchScalarGridSpec(
        num_scalar_prefetch=2,
        grid=(requests,),
        in_specs=in_specs,
        out_specs=out_specs,
    )
    return pl.pallas_call(
        functools.partial(paged_kernel, slots, chunks),
        grid_spec=grid_spec,
        out_shape=out_shape,
        cost_estimate=cost,
        compiler_params=pltpu.CompilerParams(dimension_semantics=("arbitrary",)),
        name="paged_partials",
    )(page_list, limits, queries, *([cache] * slots), draft_keys, draft_values, draft_mask)


def exchange_kernel(count, same, x_ref, out_ref, send_sems, recv_sems):
    me = lax.axis_index("rep")
    row = lax.axis_index("req")
    mesh_ids = pl.DeviceIdType.MESH
    barrier = pltpu.get_barrier_semaphore()
    for step in range(1, count):
        peer = lax.rem(me + step, count)
        pl.semaphore_signal(barrier, inc=1, device_id=(row, peer), device_id_type=mesh_ids)
    pl.semaphore_wait(barrier, count - 1)
    sends = []
    for step in range(1, count):
        peer = lax.rem(me + step, count)
        source = x_ref.at[0] if same else x_ref.at[peer]
        copy = pltpu.make_async_remote_copy(
            src_ref=source,
            dst_ref=out_ref.at[me],
            send_sem=send_sems.at[step],
            recv_sem=recv_sems.at[step],
            device_id=(row, peer),
            device_id_type=mesh_ids,
        )
        copy.start()
        sends.append(copy)
    for copy in sends:
        copy.wait_send()
    for step in range(1, count):
        origin = lax.rem(me + count - step, count)
        incoming = pltpu.make_async_remote_copy(
            src_ref=x_ref.at[0],
            dst_ref=out_ref.at[origin],
            send_sem=send_sems.at[step],
            recv_sem=recv_sems.at[step],
            device_id=(row, origin),
            device_id_type=mesh_ids,
        )
        incoming.wait_recv()


def exchange(blocks, count, same, collective_id):
    out_shape = jax.ShapeDtypeStruct((count,) + blocks.shape[1:], blocks.dtype)
    moved = blocks[0].size * blocks.dtype.itemsize * (count - 1)
    moved_in = pl.pallas_call(
        functools.partial(exchange_kernel, count, same),
        in_specs=[pl.BlockSpec(memory_space=pl.ANY)],
        out_specs=pl.BlockSpec(memory_space=pl.ANY),
        out_shape=out_shape,
        scratch_shapes=[
            pltpu.SemaphoreType.DMA((count,)),
            pltpu.SemaphoreType.DMA((count,)),
        ],
        compiler_params=pltpu.CompilerParams(collective_id=collective_id, has_side_effects=True),
        cost_estimate=pl.CostEstimate(flops=0, bytes_accessed=2 * moved, transcendentals=0),
        name=f"exchange_{collective_id}",
    )(blocks)
    me = lax.axis_index("rep")
    own = blocks[0] if same else lax.dynamic_index_in_dim(blocks, me, 0, keepdims=False)
    return lax.dynamic_update_index_in_dim(moved_in, own, me, 0)


def combine_kernel(part_ref, out_ref):
    holders, chunks = part_ref.shape[0], part_ref.shape[2]
    half = out_ref.shape[2]
    rows = 2 * half
    pieces = rows // 128
    low_h = lax.broadcasted_iota(jnp.int32, (half, 128), 1) < 64

    def as_column(row):
        column = jnp.transpose(jnp.broadcast_to(row, (128, rows)))
        return jnp.where(low_h, column[:half], column[half:])

    for c in range(chunks):
        tails = [
            part_ref[h, 0, c, half : half + 16, :].astype(jnp.float32) for h in range(holders)
        ]
        totals = [jnp.concatenate([t[p : p + 1] for p in range(pieces)], axis=1) for t in tails]
        peaks = [
            jnp.concatenate([t[pieces + p : pieces + p + 1] for p in range(pieces)], axis=1)
            + jnp.concatenate([t[2 * pieces + p : 2 * pieces + p + 1] for p in range(pieces)], axis=1)
            for t in tails
        ]
        top = peaks[0]
        for peak in peaks[1:]:
            top = jnp.maximum(top, peak)
        total = jnp.zeros_like(top)
        acc = jnp.zeros((half, 128), jnp.float32)
        for h in range(holders):
            factor = jnp.exp(peaks[h] - top)
            total = total + totals[h] * factor
            acc = acc + part_ref[h, 0, c, 0:half, :].astype(jnp.float32) * as_column(factor)
        out_ref[0, c] = (acc / as_column(total)).astype(out_ref.dtype)


def combine(parts):
    holders, requests, chunks, rows_in, lanes = parts.shape
    half = rows_in - 16
    return pl.pallas_call(
        combine_kernel,
        grid=(requests,),
        in_specs=[pl.BlockSpec((holders, 1, chunks, rows_in, lanes), lambda k: (0, k, 0, 0, 0))],
        out_specs=pl.BlockSpec((1, chunks, half, lanes), lambda k: (k, 0, 0, 0)),
        out_shape=jax.ShapeDtypeStruct((requests, chunks, half, lanes), jnp.bfloat16),
        compiler_params=pltpu.CompilerParams(dimension_semantics=("arbitrary",)),
        name="combine_holders",
    )(parts)


def finish_attention(attended, requests, tree_length):
    group = QUERY_HEADS // KEY_VALUE_HEADS
    chunks = attended.shape[1]
    shaped = attended.reshape(requests, chunks, group, tree_length, 2, 64)
    result = shaped.transpose(0, 3, 1, 4, 2, 5)
    return result.reshape(requests * tree_length, chunks * 2 * group * 64)


def rotate_flat(values, token_positions, head_columns):
    half_width = head_columns // 2
    frequency = THETA ** (-jnp.arange(half_width, dtype=jnp.float32) / half_width)
    angles = token_positions.astype(jnp.float32)[:, None] * frequency
    cosine = jnp.cos(angles)
    sines = jnp.sin(angles)
    repeats = values.shape[-1] // head_columns
    cosine = jnp.tile(jnp.concatenate([cosine, cosine], axis=-1), (1, repeats))
    sines = jnp.tile(jnp.concatenate([-sines, sines], axis=-1), (1, repeats))
    columns = jnp.arange(values.shape[-1], dtype=jnp.int32)
    front = (columns % head_columns) < half_width
    partner = jnp.where(
        front[None, :], jnp.roll(values, -half_width, axis=-1), jnp.roll(values, half_width, axis=-1)
    )
    return values * cosine + partner * sines


def body(
    hidden,
    norm_gain,
    w_qkv,
    w_out,
    ffn_gain,
    w_gate,
    w_up,
    w_down,
    cache,
    page_table,
    cache_len,
    parents,
    accept_leaf,
    page_slot,
):
    block_rows, draft_part, model_width = hidden.shape
    channels = w_qkv.shape[1]
    query_columns = w_out.shape[0]
    key_value_columns = (channels - query_columns) // 2
    req_count = lax.axis_size("req")
    rep_count = lax.axis_size("rep")
    rep_index = lax.axis_index("rep")
    requests = cache_len.shape[0]
    owner_page_count = requests // rep_count
    tree_length = parents.shape[1]
    own_start = rep_index * owner_page_count
    page_length = cache.shape[2]
    slots_count = page_table.shape[2]

    local_rows = hidden.reshape(owner_page_count, req_count, model_width)
    own_hidden = lax.all_to_all(local_rows, "req", split_axis=1, concat_axis=1, tiled=True)
    all_hidden = lax.all_gather(own_hidden, "rep", axis=0, tiled=True)

    normed = rms_scaled(all_hidden.astype(jnp.float32), norm_gain)
    projected = jnp.dot(
        normed.reshape(-1, model_width), w_qkv, preferred_element_type=jnp.float32
    ).astype(jnp.bfloat16).reshape(requests, tree_length, channels)

    reached = ancestors(parents)
    depths = jnp.sum(reached, axis=-1).astype(jnp.int32) - 1
    token_positions = cache_len[:, None] + depths
    flat_positions = token_positions.reshape(-1)
    head_columns = query_columns // QUERY_HEADS
    flat = projected.reshape(requests * tree_length, channels)
    queries = rotate_flat(
        flat[:, :query_columns].astype(jnp.float32), flat_positions, head_columns
    ).astype(jnp.bfloat16).reshape(requests, tree_length, query_columns)
    keys_all = rotate_flat(
        flat[:, query_columns : query_columns + key_value_columns].astype(jnp.float32),
        flat_positions,
        head_columns,
    ).astype(jnp.bfloat16).reshape(requests, tree_length, key_value_columns)
    values_all = projected[..., query_columns + key_value_columns :]

    page_list = page_table[:, 0, :]
    starts = (
        jnp.arange(slots_count, dtype=jnp.int32)[None, :] * rep_count + rep_index
    ) * page_length
    limits = cache_len[:, None] - starts
    mine = (jnp.arange(requests, dtype=jnp.int32) // owner_page_count) == rep_index
    draft_mask = jnp.where(mine[:, None, None], reached, 0.0)
    (parts,) = paged_partials(
        queries, cache, page_list, limits, keys_all, values_all, draft_mask
    )
    parts = parts.reshape((rep_count, owner_page_count) + parts.shape[1:])
    gathered = exchange(parts, rep_count, False, 1)
    attended = finish_attention(combine(gathered), owner_page_count, tree_length)

    mixed = jnp.dot(attended, w_out, preferred_element_type=jnp.float32)
    residual = (mixed + own_hidden.reshape(-1, model_width).astype(jnp.float32)).astype(
        jnp.bfloat16
    )
    residual_wide = residual.astype(jnp.float32)
    ffn_in = rms_scaled(residual_wide, ffn_gain).reshape(owner_page_count, tree_length, model_width)
    rows_in = exchange(ffn_in[None], rep_count, True, 2).reshape(-1, model_width)
    gate = jnp.dot(rows_in, w_gate, preferred_element_type=jnp.float32)
    up = jnp.dot(rows_in, w_up, preferred_element_type=jnp.float32)
    activated = (jax.nn.silu(gate) * up).astype(jnp.bfloat16)
    down = jnp.dot(activated, w_down, preferred_element_type=jnp.float32).reshape(
        rep_count, owner_page_count, tree_length, model_width
    )
    ffn_terms = exchange(down.astype(jnp.bfloat16), rep_count, False, 3)
    out_own = (
        jnp.sum(ffn_terms.astype(jnp.float32), axis=0)
        + residual_wide.reshape(owner_page_count, tree_length, model_width)
    ).astype(jnp.bfloat16)
    out = lax.all_to_all(out_own, "req", split_axis=1, concat_axis=1, tiled=True)
    out = out.reshape(block_rows, draft_part, model_width)

    all_rows = path_rows(keys_all, values_all, reached, depths, accept_leaf)
    new_pages = place_rows(all_rows, page_slot, own_start, owner_page_count)
    return (out, new_pages)


def solution(mesh):
    placed = (
        P("rep", "req", None),
        P(),
        P(),
        P(),
        P(),
        P(None, "rep"),
        P(None, "rep"),
        P("rep", None),
        P(("req", "rep"), None, None, None),
        P("req", "rep", None),
        P("req"),
        P("req", None),
        P("req"),
        P("req"),
    )
    return jax.shard_map(
        body,
        mesh=mesh,
        in_specs=placed,
        out_specs=(P("rep", "req", None), P(("req", "rep"), None, None, None)),
        check_vma=False,
    )
```
